256 devices in a mesh: row: 8 (over x, y_lo), col: 32 (over y_hi, z, core).
Axes of the slice: x: 4, y: 4 (y_hi: 2, y_lo: 2; y = y_hi * 2 + y_lo), z: 8, core: 2. Of those that a mesh axis runs over, the one named last changes fastest.
Arguments:
- factor: float32 [16384, 16384], P('row', 'col'), may hold values from -7 to 12
Outputs:
- factor_next: float32 [16384, 16384], P('row', 'col')
The draws below stay inside these ranges and needn't reach their ends.
All inputs are finite; a program needn't handle non-finite values.
Results may differ from the reference program's by a relative error of at most 0.0078.
Values may be sent and summed in bfloat16 or wider, within the bound.
No kernel may reach another device: no remote copies, remote signals or barrier semaphores. Data moves between devices by JAX's collectives and lax.ppermute only.
A program may use at most 64 MiB of HBM per device.

```python
import math
import jax
import jax.numpy as jnp
import numpy as np
from jax import lax

BLK = 256
SWEEPS = 2
STEPS = 2
ORDER = 16384
N_COL = 32


def draw_factor(key, part):
    key_noise = jax.random.fold_in(key, 11)
    key_diag = jax.random.fold_in(key, 12)
    key_scale = jax.random.fold_in(key, 13)
    noise_part = jnp.clip(1.8 * jax.random.normal(key_noise, (ORDER, ORDER), jnp.float32), -4.2, 4.2)
    scales = jax.random.uniform(key_scale, (ORDER,), jnp.float32, 0.95, 1.05)
    diagonal_part = jax.random.uniform(key_diag, (ORDER,), jnp.float32, 1.0, 3.0)
    symmetric = (noise_part + noise_part.T) * 0.7071 + jnp.eye(ORDER, dtype=jnp.float32) * diagonal_part[None, :]
    return symmetric * scales[:, None] * scales[None, :]


def setup_inputs(seed: int = 0) -> dict:
    key_list = jax.random.split(jax.random.key(seed), 2)
    factor = draw_factor(jax.random.fold_in(key_list[1], 71), 0)
    return dict(factor=factor)


def inner_solve(pair_block):
    size = pair_block.shape[0]
    weights = (jnp.arange(size, dtype=jnp.float32) + 1.0) / size
    step_size = 0.5 / math.sqrt(size)
    identity = jnp.eye(size, dtype=jnp.float32)
    rotation = identity
    current = pair_block
    for sweep_index in range(SWEEPS):
        skew_part = current * weights[None, :] - weights[:, None] * current
        trial_map = identity + step_size * skew_part
        gram_matrix = jnp.dot(trial_map.T, trial_map, precision=lax.Precision.HIGHEST)
        update = jnp.dot(trial_map, 1.5 * identity - 0.5 * gram_matrix, precision=lax.Precision.HIGHEST)
        current = jnp.dot(update.T, jnp.dot(current, update, precision=lax.Precision.HIGHEST), precision=lax.Precision.HIGHEST)
        rotation = jnp.dot(rotation, update, precision=lax.Precision.HIGHEST)
    return rotation

def half_sources(pair_count):
    upper = [0, 1] + [2 * (pair_index - 1) for pair_index in range(2, pair_count)]
    lower = [2 * (pair_index + 1) + 1 for pair_index in range(pair_count - 1)] + [2 * (pair_count - 1)]
    merged = []
    for pair_index in range(pair_count):
        merged += [upper[pair_index], lower[pair_index]]
    return np.array(merged)

def reference(factor):
    pair_count = N_COL
    pair_width = 2 * BLK
    sources = half_sources(pair_count)
    order_index = (sources[:, None] * BLK + np.arange(BLK)[None, :]).reshape(-1)
    matrix = factor
    for outer_step in range(STEPS):
        span = jnp.arange(pair_count)
        diagonals = matrix.reshape(pair_count, pair_width, pair_count, pair_width)[span, :, span, :]
        rotations = lax.map(inner_solve, diagonals).astype(jnp.bfloat16)
        rot_wide = rotations.astype(jnp.float32)
        lowered = matrix.astype(jnp.bfloat16).astype(jnp.float32).reshape(ORDER, pair_count, pair_width)
        right = jnp.einsum('ika,kab->ikb', lowered, rot_wide, precision=lax.Precision.HIGHEST)
        right = right.astype(jnp.bfloat16).astype(jnp.float32).reshape(pair_count, pair_width, ORDER)
        rotated = jnp.einsum('kab,kaj->kbj', rot_wide, right, precision=lax.Precision.HIGHEST)
        rotated = rotated.reshape(ORDER, ORDER)
        rotated = jnp.take(rotated, order_index, axis=0)
        matrix = jnp.take(rotated, order_index, axis=1)
    return matrix
```

```python
import math

import jax
import jax.numpy as jnp
import numpy as np
from jax import lax
from jax.experimental import pallas as pl
from jax.experimental.pallas import tpu as pltpu
from jax.sharding import Mesh
from jax.sharding import PartitionSpec as P

N = 512
H = 256
ROWS = 8
COLS = 32
GROUP = 4
ROW = ("x", "yl")
COL = ("yh", "z", "core")
ALL = ROW + COL
BF = jnp.bfloat16
F32 = jnp.float32


def dev(r, c):
    return r * COLS + c


def row_of(x, yl):
    return 2 * x + yl


def col_of(yh, z, core):
    return 16 * yh + 2 * z + core


def move(value, pairs):
    return lax.ppermute(value, ALL, pairs)


GRID = [(r, c) for r in range(ROWS) for c in range(COLS)]


def col_offset(r, c):
    return (r // 2 - c // 8) % 4, (r % 2) ^ ((c // 4) % 2)


def row_offset(r, c):
    return ((c // 2) % 8 - 2 * (r % 4)) % 8, (c // 16) ^ (r // 4)


def flag_table():
    table = np.zeros((ROWS * COLS, 16), np.int32)
    for r, c in GRID:
        local = c - GROUP * r
        dx, dy = col_offset(r, c)
        dz, dyh = row_offset(r, c)
        table[dev(r, c), :12] = [
            min(max(local, 0), GROUP - 1),
            int(0 <= local < GROUP),
            int(c == 0),
            int(c == COLS - 1),
            int(r == 0),
            int(r == ROWS - 1),
            max(c - 2, 0) % GROUP,
            dz,
            c % 2,
            dx,
            dy,
            dyh,
        ]
    return table


def x_pairs(starts, step):
    pairs = []
    for r, c in GRID:
        dx, dy = col_offset(r, c)
        if dx in starts:
            x = (r // 2 + step) % 4
            pairs.append((dev(r, c), dev(row_of(x, r % 2), c)))
    return pairs


YL_FROM_SOURCE = [(dev(k // 4, k), dev((k // 4) ^ 1, k)) for k in range(COLS)]
YL_SWAP = [(dev(r, c), dev(r ^ 1, c)) for r, c in GRID]
CORE_SWAP = [(dev(r, c), dev(r, c ^ 1)) for r, c in GRID]


def z_pairs(step, starts=None, planes=(0, 1)):
    pairs = []
    for r, c in GRID:
        dz, dyh = row_offset(r, c)
        if (starts is None or dz in starts) and dyh in planes:
            z = ((c // 2) % 8 + step) % 8
            pairs.append((dev(r, c), dev(r, col_of(c // 16, z, c % 2))))
    return pairs


YH_COPY = [(dev(r, c), dev(r, c ^ 16)) for r, c in GRID if row_offset(r, c)[1] == 0]
NEXT_DIAG = [(dev(k // 4, k), dev((k + 1) // 4, k + 1)) for k in range(COLS - 1)]
PREV_DIAG = [(dev(k // 4, k), dev((k - 1) // 4, k - 1)) for k in range(1, COLS)]
CROSS = [(dev(max(k - 1, 0) // 4, k + 1), dev(k // 4, k)) for k in range(COLS - 1)]
COL_RIGHT = [(dev(r, c), dev(r, c + 1)) for r, c in GRID if c + 1 < COLS]
COL_LEFT = [(dev(r, c), dev(r, c - 1)) for r, c in GRID if c > 0]
ROW_DOWN = [(dev(r, c), dev(r + 1, c)) for r, c in GRID if r + 1 < ROWS]
ROW_UP = [(dev(r, c), dev(r - 1, c)) for r, c in GRID if r > 0]


def mm(a, b):
    return jnp.dot(a, b, preferred_element_type=F32)


def mm_t(a, b):
    return lax.dot_general(a, b, (((0,), (0,)), ((), ())), preferred_element_type=F32)


def pair_solve(block):
    size = block.shape[0]
    step_size = 0.5 / math.sqrt(size)
    col = lax.broadcasted_iota(jnp.int32, (size, size), 1)
    row = lax.broadcasted_iota(jnp.int32, (size, size), 0)
    scale = (col - row).astype(F32) * (step_size / size)

    def small_part(current):
        skew = current * scale
        narrow = skew.astype(BF)
        excess = skew + skew.T + mm_t(narrow, narrow)
        return skew - 0.5 * (excess + mm(narrow, excess.astype(BF)))

    first = small_part(block)
    first_b = first.astype(BF)
    half_way = block + mm(block.astype(BF), first_b)
    current = half_way + mm_t(first_b, half_way.astype(BF))
    second = small_part(current)
    both = first + second + mm(first_b, second.astype(BF))
    return (both + (col == row).astype(F32)).astype(BF)


def solve_one_body(flags, block_ref, rot_ref, right_ref, left_ref):
    @pl.when(flags[1] == 1)
    def _():
        block = block_ref[...]
        rot = pair_solve(block)
        rot_ref[...] = rot
        part = mm(block.astype(BF), rot).astype(BF)
        turned = mm_t(rot, part).astype(BF)
        first = flags[2] == 1
        up = jnp.concatenate([rot[:, :H], turned[:H, :H]], 0)
        low = jnp.concatenate([rot[:, H:], turned[H:, H:]], 0)
        right_ref[...] = jnp.where(first, low, up)
        left_ref[...] = jnp.where(first, up, low)


def solve_two_body(
    flags, own_right, own_left, came_right, came_left, cross_ref, local_ref, rot_ref
):
    @pl.when(flags[1] == 1)
    def _():
        last = flags[3] == 1
        up = jnp.where(flags[2] == 1, own_left[...], came_right[...])
        low = jnp.where(last, own_right[...], came_left[...])
        cross = jnp.where(last, local_ref[...].astype(BF), cross_ref[...])
        mixed = mm_t(up[:N], mm(cross, low[:N]).astype(BF))
        block = jnp.concatenate(
            [
                jnp.concatenate([up[N:].astype(F32), mixed], 1),
                jnp.concatenate([mixed.T, low[N:].astype(F32)], 1),
            ],
            0,
        )
        rot_ref[...] = pair_solve(block)


def whole(shape):
    return pl.BlockSpec(shape, lambda i, f: (0,) * len(shape))


def call(body, flags, args, in_specs, out_specs, out_shape, grid, **kw):
    return pl.pallas_call(
        body,
        grid_spec=pltpu.PrefetchScalarGridSpec(
            num_scalar_prefetch=1, grid=grid, in_specs=in_specs, out_specs=out_specs
        ),
        out_shape=out_shape,
        compiler_params=pltpu.CompilerParams(dimension_semantics=("arbitrary",)),
        **kw,
    )(flags, *args)


def shape(*dims, dtype=BF):
    return jax.ShapeDtypeStruct(dims, dtype)


def solve_one(flags, matrix):
    return call(
        solve_one_body,
        flags,
        (matrix,),
        [pl.BlockSpec((N, N), lambda i, f: (f[0], 0))],
        [whole((N, N)), whole((N + H, H)), whole((N + H, H))],
        [shape(N, N), shape(N + H, H), shape(N + H, H)],
        (1,),
        name="solve_one",
    )


def solve_two(flags, right, left, came_right, came_left, cross, matrix):
    message = whole((N + H, H))
    return call(
        solve_two_body,
        flags,
        (right, left, came_right, came_left, cross, matrix),
        [message] * 4 + [whole((N, N)), pl.BlockSpec((N, N), lambda i, f: (GROUP - 2, 0))],
        whole((N, N)),
        shape(N, N),
        (1,),
        name="solve_two",
    )


def cast_body(flags, block_ref, out_ref):
    out_ref[...] = block_ref[...].astype(BF)


def cross_block(flags, matrix):
    return call(
        cast_body,
        flags,
        (matrix,),
        [pl.BlockSpec((N, N), lambda i, f: (f[6], 0))],
        whole((N, N)),
        shape(N, N),
        (1,),
        name="cross_block",
    )


def store_halves(flags, product, right_ref, left_ref):
    up = product[:, :H]
    low = product[:, H:]
    first = flags[2] == 1
    right_ref[...] = jnp.where(first, low, up)
    left_ref[...] = jnp.where(first, up, low)


def right_one_body(flags, block_ref, rot_ref, right_ref, left_ref):
    product = mm(block_ref[...].astype(BF), rot_ref[...]).astype(BF)
    store_halves(flags, product, right_ref, left_ref)


def right_two_body(flags, block_ref, above_ref, below_ref, rot_ref, right_ref, left_ref):
    i = pl.program_id(0)
    last = 2 * GROUP - 1
    take_above = jnp.logical_and(i == 0, flags[4] == 0)
    take_below = jnp.logical_and(i == last, flags[5] == 0)
    block = block_ref[...]
    block = jnp.where(take_above, above_ref[...], block)
    block = jnp.where(take_below, below_ref[...], block)
    product = mm(block, rot_ref[...]).astype(BF)
    store_halves(flags, product, right_ref, left_ref)


def right_one(flags, matrix, rot):
    out = pl.BlockSpec((N, H), lambda i, f: (i, 0))
    return call(
        right_one_body,
        flags,
        (matrix, rot),
        [pl.BlockSpec((N, N), lambda i, f: (i, 0)), whole((N, N))],
        [out, out],
        [shape(GROUP * N, H)] * 2,
        (GROUP,),
        name="right_one",
    )


def right_two(flags, matrix, above, below, rot):
    out = pl.BlockSpec((H, H), lambda i, f: (i, 0))
    return call(
        right_two_body,
        flags,
        (matrix, above, below, rot),
        [pl.BlockSpec((H, N), lambda i, f: (i, 0)), whole((H, N)), whole((H, N)), whole((N, N))],
        [out, out],
        [shape(GROUP * N, H)] * 2,
        (2 * GROUP,),
        name="right_two",
    )


def left_body(
    flags, own_right, own_left, came_right, came_left, mine, theirs, out_ref, down_ref, up_ref
):
    i = pl.program_id(0)
    up_in = jnp.where(flags[2] == 1, own_left[...], came_right[...])
    low_in = jnp.where(flags[3] == 1, own_right[...], came_left[...])
    block = jnp.concatenate([up_in, low_in], 1)
    own_line = (i % 2) == flags[8]
    parts = []
    for p in range(4):
        spot = lax.rem(i // 2 + 2 * p + 8 - flags[7], 8)
        parts.append(jnp.where(own_line, mine[spot], theirs[spot]))
    turned = mm_t(jnp.concatenate(parts, 0), block)
    up = turned[:H]
    low = turned[H:]
    top = flags[4] == 1

    @pl.when(i < GROUP - 1)
    def _():
        spot = jnp.where(jnp.logical_and(top, i == 0), 0, 2 * (i + 1))
        out_ref[pl.ds(spot * H, H), :] = up.astype(out_ref.dtype)

    @pl.when(i > 0)
    def _():
        spot = 2 * (i - 1) + 1
        out_ref[pl.ds(spot * H, H), :] = low.astype(out_ref.dtype)

    @pl.when(i == GROUP - 1)
    def _():
        down_ref[...] = up.astype(BF)

    @pl.when(jnp.logical_and(i == GROUP - 1, flags[5] == 1))
    def _():
        out_ref[pl.ds((2 * GROUP - 1) * H, H), :] = up.astype(out_ref.dtype)

    @pl.when(i == 0)
    def _():
        up_ref[...] = low.astype(BF)

    @pl.when(jnp.logical_and(i == 0, top))
    def _():
        out_ref[pl.ds(2 * H, H), :] = low.astype(out_ref.dtype)


def left(flags, right_own, left_own, came_right, came_left, mine, theirs, dtype):
    return call(
        left_body,
        flags,
        (right_own, left_own, came_right, came_left, mine, theirs),
        [
            pl.BlockSpec((N, H), lambda i, f: (i * f[3], 0)),
            pl.BlockSpec((N, H), lambda i, f: (i * f[2], 0)),
            pl.BlockSpec((N, H), lambda i, f: (i, 0)),
            pl.BlockSpec((N, H), lambda i, f: (i, 0)),
            whole((8, N // 4, N)),
            whole((8, N // 4, N)),
        ],
        [whole((GROUP * N, N)), whole((H, N)), whole((H, N))],
        [shape(GROUP * N, N, dtype=dtype), shape(H, N), shape(H, N)],
        (GROUP,),
        name="left",
    )


def settle_body(flags, main_ref, above_ref, below_ref, out_ref):
    i = pl.program_id(0)
    came = jnp.where(i == 0, above_ref[...], below_ref[...]).astype(F32)
    keep = jnp.where(i == 0, flags[4], flags[5]) == 1
    out_ref[...] = jnp.where(keep, main_ref[...], came)


def settle(flags, main, above, below):
    spec = pl.BlockSpec((H, N), lambda i, f: (i * (2 * GROUP - 1), 0))
    return call(
        settle_body,
        flags,
        (main, above, below),
        [spec, whole((H, N)), whole((H, N))],
        spec,
        shape(GROUP * N, N, dtype=F32),
        (2,),
        input_output_aliases={1: 0},
        name="settle",
    )


def spread_in_column(rot, dx, dy):
    q = H // 2
    sent = move(rot[H:], YL_FROM_SOURCE)
    start = jnp.where(dy == 0, rot[:H], sent)
    fore = move(start[:q], x_pairs((0,), 1))
    back = move(start[q:], x_pairs((0,), -1))
    fore_next = move(jnp.where(dx == 0, start[q:], fore), x_pairs((0, 1), 1))
    back_next = move(jnp.where(dx == 0, start[:q], back), x_pairs((0, 3), -1))
    near = jnp.where(
        dx == 0, start[:q], jnp.where(dx == 1, fore, jnp.where(dx == 2, fore_next, back_next))
    )
    far = jnp.where(
        dx == 0, start[q:], jnp.where(dx == 1, fore_next, jnp.where(dx == 2, back_next, back))
    )
    mine = jnp.concatenate([near, far], 0)
    other = move(mine, YL_SWAP)
    return jnp.concatenate(
        [jnp.where(dy == 0, mine, other), jnp.where(dy == 0, other, mine)], 0
    )


def spread_in_row(rot, dz, dyh):
    q = N // 4
    far = move(rot[2 * q :], z_pairs(4, (0, 1), (0,)))
    held = jnp.where(dz < 2, rot[: 2 * q], far)
    near = move(held[q:], z_pairs(2, (0, 1, 4, 5), (0,)))
    piece = jnp.where((dz & 2) == 0, held[:q], near)
    copied = move(piece, YH_COPY)
    piece = jnp.where(dyh == 0, piece, copied)
    fore = [piece]
    back = [piece]
    for _ in range(3):
        fore.append(move(fore[-1], z_pairs(1)))
        back.append(move(back[-1], z_pairs(-1)))
    fore_half = move(fore[3][: q // 2], z_pairs(1))
    back_half = move(back[3][q // 2 :], z_pairs(-1))
    opposite = jnp.concatenate([fore_half, back_half], 0)
    mine = jnp.stack([piece, back[1], back[2], back[3], opposite, fore[3], fore[2], fore[1]])
    return mine, move(mine, CORE_SWAP)


def shards(factor):
    x = lax.axis_index("x")
    yl = lax.axis_index("yl")
    yh = lax.axis_index("yh")
    z = lax.axis_index("z")
    core = lax.axis_index("core")
    r = 2 * x + yl
    c = 16 * yh + 2 * z + core
    dx = (x - c // 8) & 3
    dy = yl ^ ((c // 4) & 1)
    dz = (z - 2 * (r & 3)) & 7
    dyh = yh ^ (r // 4)
    flags = lax.dynamic_index_in_dim(
        jnp.asarray(flag_table()), r * COLS + c, 0, keepdims=False
    )

    cross = move(cross_block(flags, factor), CROSS)
    rot_one, to_right, to_left = solve_one(flags, factor)
    from_left = move(to_right, NEXT_DIAG)
    from_right = move(to_left, PREV_DIAG)
    rot_two = solve_two(flags, to_right, to_left, from_left, from_right, cross, factor)

    col_one = spread_in_column(rot_one, dx, dy)
    mine_one, theirs_one = spread_in_row(rot_one, dz, dyh)
    col_two = spread_in_column(rot_two, dx, dy)
    mine_two, theirs_two = spread_in_row(rot_two, dz, dyh)

    right_half, left_half = right_one(flags, factor, col_one)
    came_right = move(right_half, COL_RIGHT)
    came_left = move(left_half, COL_LEFT)
    main, down, up = left(
        flags, right_half, left_half, came_right, came_left, mine_one, theirs_one, BF
    )
    above = move(down, ROW_DOWN)
    below = move(up, ROW_UP)

    right_half, left_half = right_two(flags, main, above, below, col_two)
    came_right = move(right_half, COL_RIGHT)
    came_left = move(left_half, COL_LEFT)
    main, down, up = left(
        flags, right_half, left_half, came_right, came_left, mine_two, theirs_two, F32
    )
    above = move(down, ROW_DOWN)
    below = move(up, ROW_UP)
    return settle(flags, main, above, below)


def solution(mesh):
    split = Mesh(mesh.devices.reshape(4, 2, 2, 8, 2), ALL)
    placed = P(ROW, COL)
    return jax.shard_map(
        shards, mesh=split, in_specs=(placed,), out_specs=placed, check_vma=False
    )
```

```python
import math

import jax
import jax.numpy as jnp
import numpy as np
from jax import lax
from jax.experimental import pallas as pl
from jax.experimental.pallas import tpu as pltpu
from jax.sharding import Mesh
from jax.sharding import PartitionSpec as P

N = 512
H = 256
Q = 128
ROWS = 8
COLS = 32
GROUP = 4
ROW = ("x", "yl")
COL = ("yh", "z", "core")
ALL = ROW + COL
BF = jnp.bfloat16
F32 = jnp.float32


def dev(r, c):
    return r * COLS + c


def row_of(x, yl):
    return 2 * x + yl


def col_of(yh, z, core):
    return 16 * yh + 2 * z + core


def move(value, pairs):
    return lax.ppermute(value, ALL, pairs)


GRID = [(r, c) for r in range(ROWS) for c in range(COLS)]


def col_offset(r, c):
    return (r // 2 - c // 8) % 4, (r % 2) ^ ((c // 4) % 2)


def row_offset(r, c):
    return ((c // 2) % 8 - 2 * (r % 4)) % 8, (c // 16) ^ (r // 4)


def flag_table():
    table = np.zeros((ROWS * COLS, 16), np.int32)
    for r, c in GRID:
        local = c - GROUP * r
        dx, dy = col_offset(r, c)
        dz, dyh = row_offset(r, c)
        table[dev(r, c), :12] = [
            min(max(local, 0), GROUP - 1),
            int(0 <= local < GROUP),
            int(c == 0),
            int(c == COLS - 1),
            int(r == 0),
            int(r == ROWS - 1),
            max(c - 2, 0) % GROUP,
            dz,
            c % 2,
            dx,
            dy,
            dyh,
        ]
    return table


def x_pairs(starts, step):
    pairs = []
    for r, c in GRID:
        dx, dy = col_offset(r, c)
        if dx in starts:
            x = (r // 2 + step) % 4
            pairs.append((dev(r, c), dev(row_of(x, r % 2), c)))
    return pairs


YL_FROM_SOURCE = [(dev(k // 4, k), dev((k // 4) ^ 1, k)) for k in range(COLS)]
YL_SWAP = [(dev(r, c), dev(r ^ 1, c)) for r, c in GRID]
CORE_SWAP = [(dev(r, c), dev(r, c ^ 1)) for r, c in GRID]


def z_pairs(step, starts=None, planes=(0, 1)):
    pairs = []
    for r, c in GRID:
        dz, dyh = row_offset(r, c)
        if (starts is None or dz in starts) and dyh in planes:
            z = ((c // 2) % 8 + step) % 8
            pairs.append((dev(r, c), dev(r, col_of(c // 16, z, c % 2))))
    return pairs


SPREAD_TWO = z_pairs(-2, (0,), (0,)) + z_pairs(2, (1,), (0,))
SPREAD_ONE = z_pairs(-1, (0, 6), (0,)) + z_pairs(1, (1, 3), (0,))
YH_COPY = [(dev(r, c), dev(r, c ^ 16)) for r, c in GRID if row_offset(r, c)[1] == 0]
NEXT_DIAG = [(dev(k // 4, k), dev((k + 1) // 4, k + 1)) for k in range(COLS - 1)]
PREV_DIAG = [(dev(k // 4, k), dev((k - 1) // 4, k - 1)) for k in range(1, COLS)]
CROSS = [(dev(max(k - 1, 0) // 4, k + 1), dev(k // 4, k)) for k in range(COLS - 1)]
COL_RIGHT = [(dev(r, c), dev(r, c + 1)) for r, c in GRID if c + 1 < COLS]
COL_LEFT = [(dev(r, c), dev(r, c - 1)) for r, c in GRID if c > 0]
ROW_DOWN = [(dev(r, c), dev(r + 1, c)) for r, c in GRID if r + 1 < ROWS]
ROW_UP = [(dev(r, c), dev(r - 1, c)) for r, c in GRID if r > 0]


def mm(a, b):
    return jnp.dot(a, b, preferred_element_type=F32)


def mm_t(a, b):
    return lax.dot_general(a, b, (((0,), (0,)), ((), ())), preferred_element_type=F32)


def pair_solve(block):
    size = block.shape[0]
    step_size = 0.5 / math.sqrt(size)
    col = lax.broadcasted_iota(jnp.int32, (size, size), 1)
    row = lax.broadcasted_iota(jnp.int32, (size, size), 0)
    scale = (col - row).astype(F32) * (step_size / size)

    def small_part(current):
        skew = current * scale
        narrow = skew.astype(BF)
        excess = skew + skew.T + mm_t(narrow, narrow)
        return skew - 0.5 * (excess + mm(narrow, excess.astype(BF)))

    first = small_part(block)
    first_b = first.astype(BF)
    half_way = block + mm(block.astype(BF), first_b)
    current = half_way + mm_t(first_b, half_way.astype(BF))
    second = small_part(current)
    both = first + second + mm(first_b, second.astype(BF))
    return (both + (col == row).astype(F32)).astype(BF)


def solve_one_body(flags, block_ref, rot_ref, right_ref, left_ref):
    @pl.when(flags[1] == 1)
    def _():
        block = block_ref[...]
        rot = pair_solve(block)
        rot_ref[...] = rot
        part = mm(block.astype(BF), rot).astype(BF)
        turned = mm_t(rot, part).astype(BF)
        first = flags[2] == 1
        up = jnp.concatenate([rot[:, :H], turned[:H, :H]], 0)
        low = jnp.concatenate([rot[:, H:], turned[H:, H:]], 0)
        right_ref[...] = jnp.where(first, low, up)
        left_ref[...] = jnp.where(first, up, low)


def solve_two_body(
    flags, first_ref, own_right, own_left, came_right, came_left, cross_ref, local_ref, *outs
):
    near_ref, far_ref, near_t_ref, far_t_ref = outs

    @pl.when(flags[1] == 1)
    def _():
        last = flags[3] == 1
        up = jnp.where(flags[2] == 1, own_left[...], came_right[...])
        low = jnp.where(last, own_right[...], came_left[...])
        cross = jnp.where(last, local_ref[...].astype(BF), cross_ref[...])
        mixed = mm_t(up[:N], mm(cross, low[:N]).astype(BF))
        block = jnp.concatenate(
            [
                jnp.concatenate([up[N:].astype(F32), mixed], 1),
                jnp.concatenate([mixed.T, low[N:].astype(F32)], 1),
            ],
            0,
        )
        for slot, rot in enumerate((first_ref[...], pair_solve(block))):
            turned = rot.T
            for p in range(2):
                near_ref[p, slot] = rot[p * Q : (p + 1) * Q]
                far_ref[p, slot] = rot[H + p * Q : H + (p + 1) * Q]
                near_t_ref[p, slot] = turned[p * Q : (p + 1) * Q]
                far_t_ref[p, slot] = turned[H + p * Q : H + (p + 1) * Q]


def whole(shape):
    return pl.BlockSpec(shape, lambda i, f: (0,) * len(shape))


ANYWHERE = pl.BlockSpec(memory_space=pl.ANY)


def call(body, flags, args, in_specs, out_specs, out_shape, grid, scratch=(), **kw):
    return pl.pallas_call(
        body,
        grid_spec=pltpu.PrefetchScalarGridSpec(
            num_scalar_prefetch=1,
            grid=grid,
            in_specs=in_specs,
            out_specs=out_specs,
            scratch_shapes=scratch,
        ),
        out_shape=out_shape,
        compiler_params=pltpu.CompilerParams(dimension_semantics=("arbitrary",), vmem_limit_bytes=24 << 20
        ),
        **kw,
    )(flags, *args)


def shape(*dims, dtype=BF):
    return jax.ShapeDtypeStruct(dims, dtype)


def solve_one(flags, matrix):
    return call(
        solve_one_body,
        flags,
        (matrix,),
        [pl.BlockSpec((N, N), lambda i, f: (f[0], 0))],
        [whole((N, N))] + [whole((N + H, H))] * 2,
        [shape(N, N)] + [shape(N + H, H)] * 2,
        (1,),
        name="solve_one",
    )


def solve_two(flags, first, right, left, came_right, came_left, cross, matrix):
    message = whole((N + H, H))
    return call(
        solve_two_body,
        flags,
        (first, right, left, came_right, came_left, cross, matrix),
        [whole((N, N))] + [message] * 4 + [whole((N, N)), pl.BlockSpec((N, N), lambda i, f: (GROUP - 2, 0))],
        [whole((2, 2, Q, N))] * 4,
        [shape(2, 2, Q, N)] * 4,
        (1,),
        name="solve_two",
    )


def cast_body(flags, block_ref, out_ref):
    out_ref[...] = block_ref[...].astype(BF)


def cross_block(flags, matrix):
    return call(
        cast_body,
        flags,
        (matrix,),
        [pl.BlockSpec((N, N), lambda i, f: (f[6], 0))],
        whole((N, N)),
        shape(N, N),
        (1,),
        name="cross_block",
    )


EDGE = (0, 3)
INNER = (1, 1)


def store_halves(flags, product, right_ref, left_ref):
    up = product[:, :H]
    low = product[:, H:]
    first = flags[2] == 1
    right_ref[...] = jnp.where(first, low, up)
    left_ref[...] = jnp.where(first, up, low)


def joined(flags, own_right, own_left, came_right, came_left):
    up = jnp.where(flags[2] == 1, own_left[...], came_right[...])
    low = jnp.where(flags[3] == 1, own_right[...], came_left[...])
    return jnp.concatenate([up, low], 1)


def half_specs(base, stride):
    return [
        pl.BlockSpec((N, H), lambda i, f: ((base + stride * i) * f[3], 0)),
        pl.BlockSpec((N, H), lambda i, f: ((base + stride * i) * f[2], 0)),
        pl.BlockSpec((N, H), lambda i, f: (base + stride * i, 0)),
        pl.BlockSpec((N, H), lambda i, f: (base + stride * i, 0)),
    ]


def right_one_body(flags, block_ref, rot_ref, right_ref, left_ref):
    product = mm(block_ref[...].astype(BF), rot_ref[...].reshape(N, N)).astype(BF)
    store_halves(flags, product, right_ref, left_ref)


def right_two_body(flags, *refs):
    rot_ref, right_ref, left_ref = refs[4:]
    product = mm(joined(flags, *refs[:4]), rot_ref[...].reshape(N, N)).astype(BF)
    store_halves(flags, product, right_ref, left_ref)


def right(flags, sources, rot, slot):
    out = pl.BlockSpec((N, H), lambda i, f: (i, 0))
    first = slot == 0
    return call(
        right_one_body if first else right_two_body,
        flags,
        (*sources, rot),
        ([pl.BlockSpec((N, N), lambda i, f: (i, 0))] if first else half_specs(0, 1))
        + [pl.BlockSpec((4, 1, Q, N), lambda i, f: (0, slot, 0, 0))],
        [out, out],
        [shape(GROUP * N, H)] * 2,
        (GROUP,),
        name="right",
    )


def row_rotation(flags, i, mine, theirs):
    own_line = (i % 2) == flags[8]
    lower = i // 2
    parts = []
    for p in range(4):
        owner = jnp.where(lower == 1, 1 + p, (8 - p) % 8)
        spot = lax.rem(owner + 8 - flags[7], 8)
        parts.append(jnp.where(own_line, mine[spot, 0], theirs[spot, 0]))
    return jnp.concatenate(parts, 0)


def with_ends(flags, step, main_ref, above_ref, below_ref):
    block = main_ref[...]
    take_above = jnp.logical_and(step == 0, flags[4] == 0)
    take_below = jnp.logical_and(step == 1, flags[5] == 0)
    above = jnp.where(take_above, above_ref[...], block[:H])
    below = jnp.where(take_below, below_ref[...], block[H:])
    return jnp.concatenate([above, below], 0)


def left_body(pairs, slot, flags, *refs):
    base, stride = pairs
    step = pl.program_id(0)
    edge = pairs == EDGE
    mine, theirs = refs[:2]
    if slot == 0:
        block = joined(flags, *refs[2:6])
        rest = refs[6:]
    elif edge:
        block = with_ends(flags, step, *refs[2:5])
        rest = refs[5:]
    else:
        block = refs[2][...]
        rest = refs[3:]
    if edge:
        out_ref, down_ref, up_ref, hold, sems = rest
    else:
        out_ref, hold, sems = rest[1:]
    i = base + stride * step
    product = mm(row_rotation(flags, i, mine, theirs), block)
    up = product[:H].astype(hold.dtype)
    low = product[H:].astype(hold.dtype)
    hold[2 * step] = up
    hold[2 * step + 1] = low
    if edge:
        top = flags[4]
        up_spot = jnp.where(step == 0, 2 - 2 * top, 7)
        low_spot = jnp.where(step == 0, 2 * top, 5)

        @pl.when(step == 0)
        def _():
            up_ref[...] = low.astype(BF)

        @pl.when(step == 1)
        def _():
            down_ref[...] = up.astype(BF)
    else:
        up_spot = 2 * i + 2
        low_spot = 2 * i - 1

    def copies(s, up_at, low_at):
        return (
            pltpu.make_async_copy(
                hold.at[2 * s], out_ref.at[pl.ds(up_at * H, H), :], sems.at[2 * s]
            ),
            pltpu.make_async_copy(
                hold.at[2 * s + 1], out_ref.at[pl.ds(low_at * H, H), :], sems.at[2 * s + 1]
            ),
        )

    for copy in copies(step, up_spot, low_spot):
        copy.start()

    @pl.when(step == 1)
    def _():
        for s in range(2):
            for copy in copies(s, s, s):
                copy.wait()


def left(flags, rows, slot, pairs, sources, ends=(), target=None):
    base, stride = pairs
    edge = pairs == EDGE
    pieces = pl.BlockSpec((8, 1, Q, N), lambda i, f: (0, slot, 0, 0))
    if slot == 0:
        specs = half_specs(base, stride)
    else:
        specs = [pl.BlockSpec((N, N), lambda i, f: (base + stride * i, 0))]
    specs = specs + [whole((H, N))] * len(ends)
    dtype = BF if slot == 0 else F32
    args = (*rows, *sources, *ends)
    return call(
        lambda *refs: left_body(pairs, slot, *refs),
        flags,
        args if edge else (*args, target),
        [pieces, pieces, *specs] + ([] if edge else [ANYWHERE]),
        [ANYWHERE] + ([whole((H, N))] * 2 if edge else []),
        [shape(GROUP * N, N, dtype=dtype)] + ([shape(H, N)] * 2 if edge else []),
        (2,),
        scratch=[pltpu.VMEM((4, H, N), dtype), pltpu.SemaphoreType.DMA((4,))],
        input_output_aliases={} if edge else {len(args) + 1: 0},
        name="left_edge" if edge else "left_inner",
    )


def settle_body(flags, above_ref, below_ref, main_ref, out_ref, hold, sems):
    first = pltpu.make_async_copy(hold.at[0], out_ref.at[pl.ds(0, H), :], sems.at[0])
    last = pltpu.make_async_copy(
        hold.at[1], out_ref.at[pl.ds((2 * GROUP - 1) * H, H), :], sems.at[1]
    )

    @pl.when(flags[4] == 0)
    def _():
        hold[0] = above_ref[...].astype(F32)
        first.start()

    @pl.when(flags[5] == 0)
    def _():
        hold[1] = below_ref[...].astype(F32)
        last.start()

    @pl.when(flags[4] == 0)
    def _():
        first.wait()

    @pl.when(flags[5] == 0)
    def _():
        last.wait()


def settle(flags, main, above, below):
    return call(
        settle_body,
        flags,
        (above, below, main),
        [whole((H, N)), whole((H, N)), ANYWHERE],
        ANYWHERE,
        shape(GROUP * N, N, dtype=F32),
        (1,),
        scratch=[pltpu.VMEM((2, H, N), F32), pltpu.SemaphoreType.DMA((2,))],
        input_output_aliases={3: 0},
        name="settle",
    )


def exchange_columns(halves):
    return (*halves, move(halves[0], COL_RIGHT), move(halves[1], COL_LEFT))


def shards(factor):
    x = lax.axis_index("x")
    yl = lax.axis_index("yl")
    yh = lax.axis_index("yh")
    z = lax.axis_index("z")
    core = lax.axis_index("core")
    r = 2 * x + yl
    c = 16 * yh + 2 * z + core
    dx = (x - c // 8) & 3
    dy = yl ^ ((c // 4) & 1)
    dz = (z - 2 * (r & 3)) & 7
    dyh = yh ^ (r // 4)
    flags = lax.dynamic_index_in_dim(
        jnp.asarray(flag_table()), r * COLS + c, 0, keepdims=False
    )

    cross = move(cross_block(flags, factor), CROSS)
    rot_one, to_right, to_left = solve_one(flags, factor)
    from_left = move(to_right, NEXT_DIAG)
    from_right = move(to_left, PREV_DIAG)
    near, far, near_t, far_t = solve_two(
        flags, rot_one, to_right, to_left, from_left, from_right, cross, factor
    )
    barrier = lax.optimization_barrier

    start = jnp.where(dy == 0, near, move(far, YL_FROM_SOURCE))
    held = jnp.where(dz < 2, near_t, move(far_t, SPREAD_TWO))
    start, held = barrier((start, held))

    fore = move(start[0], x_pairs((0,), 1))
    back = move(start[1], x_pairs((0,), -1))
    nearer = move(held[1], SPREAD_ONE)
    fore_message = jnp.where(dx == 0, start[1], fore)
    back_message = jnp.where(dx == 0, start[0], back)
    take = (dz == 7) | (dz == 2) | (dz == 5) | (dz == 4)
    piece = jnp.where(take, nearer, held[0])
    fore_message, back_message, piece = barrier((fore_message, back_message, piece))

    fore_next = move(fore_message, x_pairs((0, 1), 1))
    back_next = move(back_message, x_pairs((0, 3), -1))
    copied = move(piece, YH_COPY)
    low = jnp.where(
        dx == 0, start[0], jnp.where(dx == 1, fore, jnp.where(dx == 2, fore_next, back_next))
    )
    high = jnp.where(
        dx == 0, start[1], jnp.where(dx == 1, fore_next, jnp.where(dx == 2, back_next, back))
    )
    mine = jnp.stack([low, high])
    piece = jnp.where(dyh == 0, piece, copied)
    mine, piece = barrier((mine, piece))

    other = move(mine, YL_SWAP)
    ahead = [piece]
    behind = [piece]
    for _ in range(2):
        ahead.append(move(ahead[-1], z_pairs(1)))
        behind.append(move(behind[-1], z_pairs(-1)))
    cols = jnp.concatenate(
        [jnp.where(dy == 0, mine, other), jnp.where(dy == 0, other, mine)], 0
    )
    halves = right(flags, (factor,), cols, 0)
    ahead[2], behind[2], *halves = barrier((ahead[2], behind[2], *halves))
    halves = exchange_columns(halves)
    ahead.append(move(ahead[-1], z_pairs(1)))
    behind.append(move(behind[-1], z_pairs(-1)))
    opposite = jnp.stack([move(ahead[3][0], z_pairs(1)), move(behind[3][1], z_pairs(-1))])
    line = jnp.stack([piece, *behind[1:], opposite, ahead[3], ahead[2], ahead[1]])
    rows = line, move(line, CORE_SWAP)
    halves = exchange_columns(right(flags, halves, cols, 1))

    main, down, up = left(flags, rows, 0, EDGE, halves)
    above = move(down, ROW_DOWN)
    below = move(up, ROW_UP)
    (main,) = left(flags, rows, 0, INNER, halves, target=main)
    out, down, up = left(flags, rows, 1, EDGE, (main,), (above, below))
    last_above = move(down, ROW_DOWN)
    last_below = move(up, ROW_UP)
    (out,) = left(flags, rows, 1, INNER, (main,), target=out)
    return settle(flags, out, last_above, last_below)


def solution(mesh):
    split = Mesh(mesh.devices.reshape(4, 2, 2, 8, 2), ALL)
    placed = P(ROW, COL)
    return jax.shard_map(
        shards, mesh=split, in_specs=(placed,), out_specs=placed, check_vma=False
    )
```

```python
import math

import jax
import jax.numpy as jnp
import numpy as np
from jax import lax
from jax.experimental import pallas as pl
from jax.experimental.pallas import tpu as pltpu
from jax.sharding import Mesh
from jax.sharding import PartitionSpec as P

N = 512
H = 256
Q = 128
ROWS = 8
COLS = 32
GROUP = 4
ROW = ("x", "yl")
COL = ("yh", "z", "core")
ALL = ROW + COL
BF = jnp.bfloat16
F32 = jnp.float32


def dev(r, c):
    return r * COLS + c


def row_of(x, yl):
    return 2 * x + yl


def col_of(yh, z, core):
    return 16 * yh + 2 * z + core


def move(value, pairs):
    return lax.ppermute(value, ALL, pairs)


GRID = [(r, c) for r in range(ROWS) for c in range(COLS)]


def col_offset(r, c):
    return (r // 2 - c // 8) % 4, (r % 2) ^ ((c // 4) % 2)


def row_offset(r, c):
    return ((c // 2) % 8 - 2 * (r % 4)) % 8, (c // 16) ^ (r // 4)


def flag_table():
    table = np.zeros((ROWS * COLS, 16), np.int32)
    for r, c in GRID:
        local = c - GROUP * r
        dx, dy = col_offset(r, c)
        dz, dyh = row_offset(r, c)
        table[dev(r, c), :12] = [
            min(max(local, 0), GROUP - 1),
            int(0 <= local < GROUP),
            int(c == 0),
            int(c == COLS - 1),
            int(r == 0),
            int(r == ROWS - 1),
            max(c - 2, 0) % GROUP,
            dz,
            c % 2,
            dx,
            dy,
            dyh,
        ]
    return table


def x_pairs(starts, step):
    pairs = []
    for r, c in GRID:
        dx, _ = col_offset(r, c)
        if dx in starts:
            x = (r // 2 + step) % 4
            pairs.append((dev(r, c), dev(row_of(x, r % 2), c)))
    return pairs


YL_FROM_SOURCE = [(dev(k // 4, k), dev((k // 4) ^ 1, k)) for k in range(COLS)]
YL_SWAP = [(dev(r, c), dev(r ^ 1, c)) for r, c in GRID]
CORE_SWAP = [(dev(r, c), dev(r, c ^ 1)) for r, c in GRID]


def z_pairs(step, starts=None, planes=(0, 1)):
    pairs = []
    for r, c in GRID:
        dz, dyh = row_offset(r, c)
        if (starts is None or dz in starts) and dyh in planes:
            z = ((c // 2) % 8 + step) % 8
            pairs.append((dev(r, c), dev(r, col_of(c // 16, z, c % 2))))
    return pairs


SPREAD_TWO = z_pairs(-2, (0,), (0,)) + z_pairs(2, (1,), (0,))
SPREAD_ONE = z_pairs(-1, (0, 6), (0,)) + z_pairs(1, (1, 3), (0,))
YH_COPY = [(dev(r, c), dev(r, c ^ 16)) for r, c in GRID if row_offset(r, c)[1] == 0]
NEXT_DIAG = [(dev(k // 4, k), dev((k + 1) // 4, k + 1)) for k in range(COLS - 1)]
PREV_DIAG = [(dev(k // 4, k), dev((k - 1) // 4, k - 1)) for k in range(1, COLS)]
CROSS = [(dev(max(k - 1, 0) // 4, k + 1), dev(k // 4, k)) for k in range(COLS - 1)]
COL_RIGHT = [(dev(r, c), dev(r, c + 1)) for r, c in GRID if c + 1 < COLS]
COL_LEFT = [(dev(r, c), dev(r, c - 1)) for r, c in GRID if c > 0]
ROW_DOWN = [(dev(r, c), dev(r + 1, c)) for r, c in GRID if r + 1 < ROWS]
ROW_UP = [(dev(r, c), dev(r - 1, c)) for r, c in GRID if r > 0]


def mm(a, b):
    return jnp.dot(a, b, preferred_element_type=F32)


def mm_t(a, b):
    return lax.dot_general(a, b, (((0,), (0,)), ((), ())), preferred_element_type=F32)


def pair_solve(block):
    size = block.shape[0]
    step_size = 0.5 / math.sqrt(size)
    col = lax.broadcasted_iota(jnp.int32, (size, size), 1)
    row = lax.broadcasted_iota(jnp.int32, (size, size), 0)
    scale = (col - row).astype(F32) * (step_size / size)

    def small_part(current):
        skew = current * scale
        narrow = skew.astype(BF)
        excess = skew + skew.T + mm_t(narrow, narrow)
        return skew - 0.5 * (excess + mm(narrow, excess.astype(BF)))

    first = small_part(block)
    first_b = first.astype(BF)
    half_way = block + mm(block.astype(BF), first_b)
    current = half_way + mm_t(first_b, half_way.astype(BF))
    second = small_part(current)
    both = first + second + mm(first_b, second.astype(BF))
    return (both + (col == row).astype(F32)).astype(BF)


def store_rotation(rot, near_ref, far_ref, near_t_ref, far_t_ref):
    turned = rot.T
    for p in range(2):
        near_ref[p] = rot[p * Q : (p + 1) * Q]
        far_ref[p] = rot[H + p * Q : H + (p + 1) * Q]
        near_t_ref[p] = turned[p * Q : (p + 1) * Q]
        far_t_ref[p] = turned[H + p * Q : H + (p + 1) * Q]


def solve_one_body(
    flags, matrix_ref, near, far, near_t, far_t, right_ref, left_ref, hold, sem
):
    @pl.when(flags[1] == 1)
    def _():
        fetched(matrix_ref, flags[0], hold, sem)
        block = hold[...]
        rot = pair_solve(block)
        store_rotation(rot, near, far, near_t, far_t)
        part = mm(block.astype(BF), rot).astype(BF)
        turned = mm_t(rot, part).astype(BF)
        first = flags[2] == 1
        up = jnp.concatenate([rot[:, :H], turned[:H, :H]], 0)
        low = jnp.concatenate([rot[:, H:], turned[H:, H:]], 0)
        right_ref[...] = jnp.where(first, low, up)
        left_ref[...] = jnp.where(first, up, low)


def solve_two_body(
    flags, own_right, own_left, came_right, came_left, cross_ref, last_ref, *outs
):
    @pl.when(flags[1] == 1)
    def _():
        last = flags[3] == 1
        up = jnp.where(flags[2] == 1, own_left[...], came_right[...])
        low = jnp.where(last, own_right[...], came_left[...])
        cross = jnp.where(last, last_ref[...], cross_ref[...])
        mixed = mm_t(up[:N], mm(cross, low[:N]).astype(BF))
        block = jnp.concatenate(
            [
                jnp.concatenate([up[N:].astype(F32), mixed], 1),
                jnp.concatenate([mixed.T, low[N:].astype(F32)], 1),
            ],
            0,
        )
        store_rotation(pair_solve(block), *outs)


def whole(shape):
    return pl.BlockSpec(shape, lambda i, f: (0,) * len(shape))


ANYWHERE = pl.BlockSpec(memory_space=pl.ANY)
IN_HBM = pl.BlockSpec(memory_space=pltpu.MemorySpace.HBM)
FETCH = [pltpu.VMEM((N, N), F32), pltpu.SemaphoreType.DMA]


def call(body, flags, args, in_specs, out_specs, out_shape, grid, scratch=(), **kw):
    return pl.pallas_call(
        body,
        grid_spec=pltpu.PrefetchScalarGridSpec(
            num_scalar_prefetch=1,
            grid=grid,
            in_specs=in_specs,
            out_specs=out_specs,
            scratch_shapes=scratch,
        ),
        out_shape=out_shape,
        compiler_params=pltpu.CompilerParams(dimension_semantics=("arbitrary",), vmem_limit_bytes=24 << 20
        ),
        **kw,
    )(flags, *args)


def shape(*dims, dtype=BF):
    return jax.ShapeDtypeStruct(dims, dtype)


def solve_one(flags, matrix):
    return call(
        solve_one_body,
        flags,
        (matrix,),
        [IN_HBM],
        [whole((2, Q, N))] * 4 + [whole((N + H, H))] * 2,
        [shape(2, Q, N)] * 4 + [shape(N + H, H)] * 2,
        (1,),
        scratch=FETCH,
        name="solve_one",
    )


def solve_two(flags, right, left, came_right, came_left, cross, last):
    message = whole((N + H, H))
    return call(
        solve_two_body,
        flags,
        (right, left, came_right, came_left, cross, last),
        [message] * 4 + [whole((N, N))] * 2,
        [whole((2, Q, N))] * 4,
        [shape(2, Q, N)] * 4,
        (1,),
        name="solve_two",
    )


def fetched(matrix_ref, slot, hold, sem):
    copy = pltpu.make_async_copy(matrix_ref.at[pl.ds(slot * N, N), :], hold, sem)
    copy.start()
    copy.wait()


def cast_body(flags, matrix_ref, out_ref, last_ref, hold, sem):
    fetched(matrix_ref, flags[6], hold, sem)
    out_ref[...] = hold[...].astype(BF)

    @pl.when(flags[3] == 1)
    def _():
        fetched(matrix_ref, GROUP - 2, hold, sem)
        last_ref[...] = hold[...].astype(BF)


def cross_block(flags, matrix):
    return call(
        cast_body,
        flags,
        (matrix,),
        [IN_HBM],
        [whole((N, N))] * 2,
        [shape(N, N)] * 2,
        (1,),
        scratch=FETCH,
        name="cross_block",
    )


EDGE = (0, 3)
INNER = (1, 1)


def store_halves(flags, product, right_ref, left_ref):
    up = product[:, :H]
    low = product[:, H:]
    first = flags[2] == 1
    right_ref[...] = jnp.where(first, low, up)
    left_ref[...] = jnp.where(first, up, low)


def joined(flags, own_right, own_left, came_right, came_left):
    up = jnp.where(flags[2] == 1, own_left[...], came_right[...])
    low = jnp.where(flags[3] == 1, own_right[...], came_left[...])
    return jnp.concatenate([up, low], 1)


def half_specs(base, stride):
    return [
        pl.BlockSpec((N, H), lambda i, f: ((base + stride * i) * f[3], 0)),
        pl.BlockSpec((N, H), lambda i, f: ((base + stride * i) * f[2], 0)),
        pl.BlockSpec((N, H), lambda i, f: (base + stride * i, 0)),
        pl.BlockSpec((N, H), lambda i, f: (base + stride * i, 0)),
    ]


def right_one_body(flags, block_ref, rot_ref, right_ref, left_ref):
    product = mm(block_ref[...].astype(BF), rot_ref[...].reshape(N, N)).astype(BF)
    store_halves(flags, product, right_ref, left_ref)


def right_two_body(flags, *refs):
    rot_ref, right_ref, left_ref = refs[4:]
    product = mm(joined(flags, *refs[:4]), rot_ref[...].reshape(N, N)).astype(BF)
    store_halves(flags, product, right_ref, left_ref)


def right(flags, sources, rot, slot):
    out = pl.BlockSpec((N, H), lambda i, f: (i, 0))
    first = slot == 0
    return call(
        right_one_body if first else right_two_body,
        flags,
        (*sources, rot),
        ([pl.BlockSpec((N, N), lambda i, f: (i, 0))] if first else half_specs(0, 1))
        + [pl.BlockSpec((4, 1, Q, N), lambda i, f: (0, slot, 0, 0))],
        [out, out],
        [shape(GROUP * N, H)] * 2,
        (GROUP,),
        name="right",
    )


def row_rotation(flags, i, mine, theirs):
    own_line = (i % 2) == flags[8]
    lower = i // 2
    parts = []
    for p in range(4):
        owner = jnp.where(lower == 1, 1 + p, (8 - p) % 8)
        spot = lax.rem(owner + 8 - flags[7], 8)
        parts.append(jnp.where(own_line, mine[spot, 0], theirs[spot, 0]))
    return jnp.concatenate(parts, 0)


def with_ends(flags, step, main_ref, above_ref, below_ref):
    block = main_ref[...]
    take_above = jnp.logical_and(step == 0, flags[4] == 0)
    take_below = jnp.logical_and(step == 1, flags[5] == 0)
    above = jnp.where(take_above, above_ref[...], block[:H])
    below = jnp.where(take_below, below_ref[...], block[H:])
    return jnp.concatenate([above, below], 0)


def left_body(pairs, slot, flags, *refs):
    base, stride = pairs
    step = pl.program_id(0)
    edge = pairs == EDGE
    mine, theirs = refs[:2]
    if slot == 0:
        block = joined(flags, *refs[2:6])
        rest = refs[6:]
    elif edge:
        block = with_ends(flags, step, *refs[2:5])
        rest = refs[5:]
    else:
        block = refs[2][...]
        rest = refs[3:]
    if edge:
        out_ref, down_ref, up_ref, hold, sems = rest
    else:
        out_ref, hold, sems = rest[1:]
    i = base + stride * step
    product = mm(row_rotation(flags, i, mine, theirs), block)
    up = product[:H].astype(hold.dtype)
    low = product[H:].astype(hold.dtype)
    hold[2 * step] = up
    hold[2 * step + 1] = low
    if edge:
        top = flags[4]
        up_spot = jnp.where(step == 0, 2 - 2 * top, 7)
        low_spot = jnp.where(step == 0, 2 * top, 5)

        @pl.when(step == 0)
        def _():
            up_ref[...] = low.astype(BF)

        @pl.when(step == 1)
        def _():
            down_ref[...] = up.astype(BF)
    else:
        up_spot = 2 * i + 2
        low_spot = 2 * i - 1

    def copies(s, up_at, low_at):
        return (
            pltpu.make_async_copy(
                hold.at[2 * s], out_ref.at[pl.ds(up_at * H, H), :], sems.at[2 * s]
            ),
            pltpu.make_async_copy(
                hold.at[2 * s + 1], out_ref.at[pl.ds(low_at * H, H), :], sems.at[2 * s + 1]
            ),
        )

    for copy in copies(step, up_spot, low_spot):
        copy.start()

    @pl.when(step == 1)
    def _():
        for s in range(2):
            for copy in copies(s, s, s):
                copy.wait()


def left(flags, rows, slot, pairs, sources, ends=(), target=None):
    base, stride = pairs
    edge = pairs == EDGE
    pieces = pl.BlockSpec((8, 1, Q, N), lambda i, f: (0, slot, 0, 0))
    if slot == 0:
        specs = half_specs(base, stride)
    else:
        specs = [pl.BlockSpec((N, N), lambda i, f: (base + stride * i, 0))]
    specs = specs + [whole((H, N))] * len(ends)
    dtype = BF if slot == 0 else F32
    args = (*rows, *sources, *ends)
    return call(
        lambda *refs: left_body(pairs, slot, *refs),
        flags,
        args if edge else (*args, target),
        [pieces, pieces, *specs] + ([] if edge else [ANYWHERE]),
        [ANYWHERE] + ([whole((H, N))] * 2 if edge else []),
        [shape(GROUP * N, N, dtype=dtype)] + ([shape(H, N)] * 2 if edge else []),
        (2,),
        scratch=[pltpu.VMEM((4, H, N), dtype), pltpu.SemaphoreType.DMA((4,))],
        input_output_aliases={} if edge else {len(args) + 1: 0},
        name="left_edge" if edge else "left_inner",
    )


def settle_body(flags, above_ref, below_ref, main_ref, out_ref, hold, sems):
    first = pltpu.make_async_copy(hold.at[0], out_ref.at[pl.ds(0, H), :], sems.at[0])
    last = pltpu.make_async_copy(
        hold.at[1], out_ref.at[pl.ds((2 * GROUP - 1) * H, H), :], sems.at[1]
    )

    @pl.when(flags[4] == 0)
    def _():
        hold[0] = above_ref[...].astype(F32)
        first.start()

    @pl.when(flags[5] == 0)
    def _():
        hold[1] = below_ref[...].astype(F32)
        last.start()

    @pl.when(flags[4] == 0)
    def _():
        first.wait()

    @pl.when(flags[5] == 0)
    def _():
        last.wait()


def settle(flags, main, above, below):
    return call(
        settle_body,
        flags,
        (above, below, main),
        [whole((H, N)), whole((H, N)), ANYWHERE],
        ANYWHERE,
        shape(GROUP * N, N, dtype=F32),
        (1,),
        scratch=[pltpu.VMEM((2, H, N), F32), pltpu.SemaphoreType.DMA((2,))],
        input_output_aliases={3: 0},
        name="settle",
    )


def exchange_columns(halves):
    return (*halves, move(halves[0], COL_RIGHT), move(halves[1], COL_LEFT))


def steps(factor):
    x = lax.axis_index("x")
    yl = lax.axis_index("yl")
    yh = lax.axis_index("yh")
    z = lax.axis_index("z")
    core = lax.axis_index("core")
    r = 2 * x + yl
    c = 16 * yh + 2 * z + core
    dx = (x - c // 8) & 3
    dy = yl ^ ((c // 4) & 1)
    dz = (z - 2 * (r & 3)) & 7
    dyh = yh ^ (r // 4)
    flags = lax.dynamic_index_in_dim(
        jnp.asarray(flag_table()), r * COLS + c, 0, keepdims=False
    )

    cross_out, cross_last = cross_block(flags, factor)
    cross = move(cross_out, CROSS)
    *rot_one, to_right, to_left = solve_one(flags, factor)
    from_left = move(to_right, NEXT_DIAG)
    from_right = move(to_left, PREV_DIAG)

    def out_of_source(rot):
        near, far, near_t, far_t = rot
        held = jnp.where(dz < 2, near_t, move(far_t, SPREAD_TWO))
        start = jnp.where(dy == 0, near, move(far, YL_FROM_SOURCE))
        return start, held

    sent_one = out_of_source(rot_one)
    rot_two = solve_two(flags, to_right, to_left, from_left, from_right, cross, cross_last)
    sent_two = out_of_source(rot_two)
    start = jnp.stack([sent_one[0], sent_two[0]], 1)
    held = jnp.stack([sent_one[1], sent_two[1]], 1)

    nearer = move(held[1], SPREAD_ONE)
    fore = move(start[0], x_pairs((0,), 1))
    back = move(start[1], x_pairs((0,), -1))
    fore_message = jnp.where(dx == 0, start[1], fore)
    back_message = jnp.where(dx == 0, start[0], back)
    take = (dz == 7) | (dz == 2) | (dz == 5) | (dz == 4)
    piece = jnp.where(take, nearer, held[0])

    copied = move(piece, YH_COPY)
    fore_next = move(fore_message, x_pairs((0, 1), 1))
    back_next = move(back_message, x_pairs((0, 3), -1))
    low = jnp.where(
        dx == 0, start[0], jnp.where(dx == 1, fore, jnp.where(dx == 2, fore_next, back_next))
    )
    high = jnp.where(
        dx == 0, start[1], jnp.where(dx == 1, fore_next, jnp.where(dx == 2, back_next, back))
    )
    mine = jnp.stack([low, high])
    piece = jnp.where(dyh == 0, piece, copied)

    other = move(mine, YL_SWAP)
    ahead = [piece]
    behind = [piece]

    def ring():
        ahead.append(move(ahead[-1], z_pairs(1)))
        behind.append(move(behind[-1], z_pairs(-1)))

    ring()
    ring()
    cols = jnp.concatenate(
        [jnp.where(dy == 0, mine, other), jnp.where(dy == 0, other, mine)], 0
    )
    halves = right(flags, (factor,), cols, 0)
    ring()
    halves = exchange_columns(halves)
    last = (move(ahead[3][0], z_pairs(1)), move(behind[3][1], z_pairs(-1)))
    halves = right(flags, halves, cols, 1)
    halves = exchange_columns(halves)
    line = jnp.stack(
        [piece, *behind[1:], jnp.stack(last), ahead[3], ahead[2], ahead[1]]
    )
    rows = line, move(line, CORE_SWAP)

    main, down, up = left(flags, rows, 0, EDGE, halves)
    above = move(down, ROW_DOWN)
    below = move(up, ROW_UP)
    (main,) = left(flags, rows, 0, INNER, halves, target=main)
    out, down, up = left(flags, rows, 1, EDGE, (main,), (above, below))
    last_above = move(down, ROW_DOWN)
    last_below = move(up, ROW_UP)
    (out,) = left(flags, rows, 1, INNER, (main,), target=out)
    return settle(flags, out, last_above, last_below)


def solution(mesh):
    split = Mesh(mesh.devices.reshape(4, 2, 2, 8, 2), ALL)
    placed = P(ROW, COL)
    return jax.shard_map(
        steps, mesh=split, in_specs=(placed,), out_specs=placed, check_vma=False
    )
```

```python
import math

import jax
import jax.numpy as jnp
import numpy as np
from jax import lax
from jax.experimental import pallas as pl
from jax.experimental.pallas import tpu as pltpu
from jax.sharding import Mesh
from jax.sharding import PartitionSpec as P

N = 512
H = 256
Q = 128
ROWS = 8
COLS = 32
GROUP = 4
ROW = ("x", "yl")
COL = ("yh", "z", "core")
ALL = ROW + COL
BF = jnp.bfloat16
F32 = jnp.float32


def dev(r, c):
    return r * COLS + c


def row_of(x, yl):
    return 2 * x + yl


def col_of(yh, z, core):
    return 16 * yh + 2 * z + core


def move(value, pairs):
    return lax.ppermute(value, ALL, pairs)


GRID = [(r, c) for r in range(ROWS) for c in range(COLS)]


def col_offset(r, c):
    return (r // 2 - c // 8) % 4, (r % 2) ^ ((c // 4) % 2)


def row_offset(r, c):
    return ((c // 2) % 8 - 2 * (r % 4)) % 8, (c // 16) ^ (r // 4)


def flag_table():
    table = np.zeros((ROWS * COLS, 16), np.int32)
    for r, c in GRID:
        local = c - GROUP * r
        dx, dy = col_offset(r, c)
        dz, dyh = row_offset(r, c)
        table[dev(r, c), :12] = [
            min(max(local, 0), GROUP - 1),
            int(0 <= local < GROUP),
            int(c == 0),
            int(c == COLS - 1),
            int(r == 0),
            int(r == ROWS - 1),
            max(c - 2, 0) % GROUP,
            dz,
            c % 2,
            dx,
            dy,
            dyh,
        ]
    return table


def x_pairs(starts, step):
    pairs = []
    for r, c in GRID:
        dx, _ = col_offset(r, c)
        if dx in starts:
            x = (r // 2 + step) % 4
            pairs.append((dev(r, c), dev(row_of(x, r % 2), c)))
    return pairs


YL_FROM_SOURCE = [(dev(k // 4, k), dev((k // 4) ^ 1, k)) for k in range(COLS)]
YL_SWAP = [(dev(r, c), dev(r ^ 1, c)) for r, c in GRID]
CORE_SWAP = [(dev(r, c), dev(r, c ^ 1)) for r, c in GRID]


def z_pairs(step, starts=None, planes=(0, 1)):
    pairs = []
    for r, c in GRID:
        dz, dyh = row_offset(r, c)
        if (starts is None or dz in starts) and dyh in planes:
            z = ((c // 2) % 8 + step) % 8
            pairs.append((dev(r, c), dev(r, col_of(c // 16, z, c % 2))))
    return pairs


SPREAD_TWO = z_pairs(-2, (0,), (0,)) + z_pairs(2, (1,), (0,))
SPREAD_ONE = z_pairs(-1, (0, 6), (0,)) + z_pairs(1, (1, 3), (0,))
YH_COPY = [(dev(r, c), dev(r, c ^ 16)) for r, c in GRID if row_offset(r, c)[1] == 0]
NEXT_DIAG = [(dev(k // 4, k), dev((k + 1) // 4, k + 1)) for k in range(COLS - 1)]
PREV_DIAG = [(dev(k // 4, k), dev((k - 1) // 4, k - 1)) for k in range(1, COLS)]
CROSS = [(dev(max(k - 1, 0) // 4, k + 1), dev(k // 4, k)) for k in range(COLS - 1)]
COL_RIGHT = [(dev(r, c), dev(r, c + 1)) for r, c in GRID if c + 1 < COLS]
COL_LEFT = [(dev(r, c), dev(r, c - 1)) for r, c in GRID if c > 0]
ROW_DOWN = [(dev(r, c), dev(r + 1, c)) for r, c in GRID if r + 1 < ROWS]
ROW_UP = [(dev(r, c), dev(r - 1, c)) for r, c in GRID if r > 0]


def mm(a, b):
    return jnp.dot(a, b, preferred_element_type=F32)


def mm_t(a, b):
    return lax.dot_general(a, b, (((0,), (0,)), ((), ())), preferred_element_type=F32)


def pair_solve(block):
    size = block.shape[0]
    step_size = 0.5 / math.sqrt(size)
    col = lax.broadcasted_iota(jnp.int32, (size, size), 1)
    row = lax.broadcasted_iota(jnp.int32, (size, size), 0)
    scale = (col - row).astype(F32) * (step_size / size)

    def small_part(current):
        skew = current * scale
        narrow = skew.astype(BF)
        excess = skew + skew.T + mm_t(narrow, narrow)
        return skew - 0.5 * (excess + mm(narrow, excess.astype(BF)))

    first = small_part(block)
    first_b = first.astype(BF)
    half_way = block + mm(block.astype(BF), first_b)
    current = half_way + mm_t(first_b, half_way.astype(BF))
    second = small_part(current)
    both = first + second + mm(first_b, second.astype(BF))
    return (both + (col == row).astype(F32)).astype(BF)


def store_rotation(rot, near_ref, far_ref, near_t_ref, far_t_ref):
    turned = rot.T
    for p in range(2):
        near_ref[p] = rot[p * Q : (p + 1) * Q]
        far_ref[p] = rot[H + p * Q : H + (p + 1) * Q]
        near_t_ref[p] = turned[p * Q : (p + 1) * Q]
        far_t_ref[p] = turned[H + p * Q : H + (p + 1) * Q]


def solve_one_body(
    flags, matrix_ref, near, far, near_t, far_t, right_ref, left_ref, hold, sem
):
    @pl.when(flags[1] == 1)
    def _():
        fetched(matrix_ref, flags[0], hold, sem)
        block = hold[...]
        rot = pair_solve(block)
        store_rotation(rot, near, far, near_t, far_t)
        part = mm(block.astype(BF), rot).astype(BF)
        turned = mm_t(rot, part).astype(BF)
        first = flags[2] == 1
        up = jnp.concatenate([rot[:, :H], turned[:H, :H]], 0)
        low = jnp.concatenate([rot[:, H:], turned[H:, H:]], 0)
        right_ref[...] = jnp.where(first, low, up)
        left_ref[...] = jnp.where(first, up, low)


def solve_two_body(
    flags, own_right, own_left, came_right, came_left, cross_ref, last_ref, *outs
):
    @pl.when(flags[1] == 1)
    def _():
        last = flags[3] == 1
        up = jnp.where(flags[2] == 1, own_left[...], came_right[...])
        low = jnp.where(last, own_right[...], came_left[...])
        cross = jnp.where(last, last_ref[...], cross_ref[...])
        mixed = mm_t(up[:N], mm(cross, low[:N]).astype(BF))
        block = jnp.concatenate(
            [
                jnp.concatenate([up[N:].astype(F32), mixed], 1),
                jnp.concatenate([mixed.T, low[N:].astype(F32)], 1),
            ],
            0,
        )
        store_rotation(pair_solve(block), *outs)


def whole(shape):
    return pl.BlockSpec(shape, lambda i, f: (0,) * len(shape))


ANYWHERE = pl.BlockSpec(memory_space=pl.ANY)
IN_HBM = pl.BlockSpec(memory_space=pltpu.MemorySpace.HBM)
FETCH = [pltpu.VMEM((N, N), F32), pltpu.SemaphoreType.DMA]


def call(body, flags, args, in_specs, out_specs, out_shape, grid, scratch=(), **kw):
    return pl.pallas_call(
        body,
        grid_spec=pltpu.PrefetchScalarGridSpec(
            num_scalar_prefetch=1,
            grid=grid,
            in_specs=in_specs,
            out_specs=out_specs,
            scratch_shapes=scratch,
        ),
        out_shape=out_shape,
        compiler_params=pltpu.CompilerParams(dimension_semantics=("arbitrary",), vmem_limit_bytes=24 << 20
        ),
        **kw,
    )(flags, *args)


def shape(*dims, dtype=BF):
    return jax.ShapeDtypeStruct(dims, dtype)


def solve_one(flags, matrix):
    return call(
        solve_one_body,
        flags,
        (matrix,),
        [IN_HBM],
        [whole((2, Q, N))] * 4 + [whole((N + H, H))] * 2,
        [shape(2, Q, N)] * 4 + [shape(N + H, H)] * 2,
        (1,),
        scratch=FETCH,
        name="solve_one",
    )


def solve_two(flags, right, left, came_right, came_left, cross, last):
    message = whole((N + H, H))
    return call(
        solve_two_body,
        flags,
        (right, left, came_right, came_left, cross, last),
        [message] * 4 + [whole((N, N))] * 2,
        [whole((2, Q, N))] * 4,
        [shape(2, Q, N)] * 4,
        (1,),
        name="solve_two",
    )


def fetched(matrix_ref, slot, hold, sem):
    copy = pltpu.make_async_copy(matrix_ref.at[pl.ds(slot * N, N), :], hold, sem)
    copy.start()
    copy.wait()


def cast_body(flags, matrix_ref, out_ref, last_ref, hold, sem):
    fetched(matrix_ref, flags[6], hold, sem)
    out_ref[...] = hold[...].astype(BF)

    @pl.when(flags[3] == 1)
    def _():
        fetched(matrix_ref, GROUP - 2, hold, sem)
        last_ref[...] = hold[...].astype(BF)


def cross_block(flags, matrix):
    return call(
        cast_body,
        flags,
        (matrix,),
        [IN_HBM],
        [whole((N, N))] * 2,
        [shape(N, N)] * 2,
        (1,),
        scratch=FETCH,
        name="cross_block",
    )


EDGE = (0, 3)
INNER = (1, 1)


def store_halves(flags, product, right_ref, left_ref):
    up = product[:, :H]
    low = product[:, H:]
    first = flags[2] == 1
    right_ref[...] = jnp.where(first, low, up)
    left_ref[...] = jnp.where(first, up, low)


def joined(flags, own_right, own_left, came_right, came_left):
    up = jnp.where(flags[2] == 1, own_left[...], came_right[...])
    low = jnp.where(flags[3] == 1, own_right[...], came_left[...])
    return jnp.concatenate([up, low], 1)


def half_specs(base, stride):
    return [
        pl.BlockSpec((N, H), lambda i, f: ((base + stride * i) * f[3], 0)),
        pl.BlockSpec((N, H), lambda i, f: ((base + stride * i) * f[2], 0)),
        pl.BlockSpec((N, H), lambda i, f: (base + stride * i, 0)),
        pl.BlockSpec((N, H), lambda i, f: (base + stride * i, 0)),
    ]


def right_one_body(flags, block_ref, rot_ref, right_ref, left_ref):
    product = mm(block_ref[...].astype(BF), rot_ref[...].reshape(N, N)).astype(BF)
    store_halves(flags, product, right_ref, left_ref)


def right_two_body(flags, *refs):
    rot_ref, right_ref, left_ref = refs[4:]
    product = mm(joined(flags, *refs[:4]), rot_ref[...].reshape(N, N)).astype(BF)
    store_halves(flags, product, right_ref, left_ref)


def right(flags, sources, rot, slot, pairs):
    base, stride = pairs
    out = pl.BlockSpec((N, H), lambda i, f: (i, 0))
    first = slot == 0
    return call(
        right_one_body if first else right_two_body,
        flags,
        (*sources, rot),
        (
            [pl.BlockSpec((N, N), lambda i, f: (base + stride * i, 0))]
            if first
            else half_specs(0, 1)
        )
        + [pl.BlockSpec((4, 1, Q, N), lambda i, f: (0, slot, 0, 0))],
        [out, out],
        [shape(2 * N, H)] * 2,
        (2,),
        name="right",
    )


def row_rotation(flags, i, mine, theirs):
    own_line = (i % 2) == flags[8]
    lower = i // 2
    parts = []
    for p in range(4):
        owner = jnp.where(lower == 1, 1 + p, (8 - p) % 8)
        spot = lax.rem(owner + 8 - flags[7], 8)
        parts.append(jnp.where(own_line, mine[spot, 0], theirs[spot, 0]))
    return jnp.concatenate(parts, 0)


def with_ends(flags, step, main_ref, above_ref, below_ref):
    block = main_ref[...]
    take_above = jnp.logical_and(step == 0, flags[4] == 0)
    take_below = jnp.logical_and(step == 1, flags[5] == 0)
    above = jnp.where(take_above, above_ref[...], block[:H])
    below = jnp.where(take_below, below_ref[...], block[H:])
    return jnp.concatenate([above, below], 0)


def left_body(pairs, slot, flags, *refs):
    base, stride = pairs
    step = pl.program_id(0)
    edge = pairs == EDGE
    mine, theirs = refs[:2]
    if slot == 0:
        block = joined(flags, *refs[2:6])
        rest = refs[6:]
    elif edge:
        block = with_ends(flags, step, *refs[2:5])
        rest = refs[5:]
    else:
        block = refs[2][...]
        rest = refs[3:]
    if edge:
        out_ref, down_ref, up_ref, hold, sems = rest
    else:
        out_ref, hold, sems = rest[1:]
    i = base + stride * step
    product = mm(row_rotation(flags, i, mine, theirs), block)
    up = product[:H].astype(hold.dtype)
    low = product[H:].astype(hold.dtype)
    hold[2 * step] = up
    hold[2 * step + 1] = low
    if edge:
        top = flags[4]
        up_spot = jnp.where(step == 0, 2 - 2 * top, 7)
        low_spot = jnp.where(step == 0, 2 * top, 5)

        @pl.when(step == 0)
        def _():
            up_ref[...] = low.astype(BF)

        @pl.when(step == 1)
        def _():
            down_ref[...] = up.astype(BF)
    else:
        up_spot = 2 * i + 2
        low_spot = 2 * i - 1

    def copies(s, up_at, low_at):
        return (
            pltpu.make_async_copy(
                hold.at[2 * s], out_ref.at[pl.ds(up_at * H, H), :], sems.at[2 * s]
            ),
            pltpu.make_async_copy(
                hold.at[2 * s + 1], out_ref.at[pl.ds(low_at * H, H), :], sems.at[2 * s + 1]
            ),
        )

    for copy in copies(step, up_spot, low_spot):
        copy.start()

    @pl.when(step == 1)
    def _():
        for s in range(2):
            for copy in copies(s, s, s):
                copy.wait()


def left(flags, rows, slot, pairs, sources, ends=(), target=None):
    base, stride = pairs
    edge = pairs == EDGE
    pieces = pl.BlockSpec((8, 1, Q, N), lambda i, f: (0, slot, 0, 0))
    if slot == 0:
        specs = half_specs(0, 1)
    else:
        specs = [pl.BlockSpec((N, N), lambda i, f: (base + stride * i, 0))]
    specs = specs + [whole((H, N))] * len(ends)
    dtype = BF if slot == 0 else F32
    args = (*rows, *sources, *ends)
    return call(
        lambda *refs: left_body(pairs, slot, *refs),
        flags,
        args if edge else (*args, target),
        [pieces, pieces, *specs] + ([] if edge else [ANYWHERE]),
        [ANYWHERE] + ([whole((H, N))] * 2 if edge else []),
        [shape(GROUP * N, N, dtype=dtype)] + ([shape(H, N)] * 2 if edge else []),
        (2,),
        scratch=[pltpu.VMEM((4, H, N), dtype), pltpu.SemaphoreType.DMA((4,))],
        input_output_aliases={} if edge else {len(args) + 1: 0},
        name="left_edge" if edge else "left_inner",
    )


def settle_body(flags, above_ref, below_ref, main_ref, out_ref, hold, sems):
    first = pltpu.make_async_copy(hold.at[0], out_ref.at[pl.ds(0, H), :], sems.at[0])
    last = pltpu.make_async_copy(
        hold.at[1], out_ref.at[pl.ds((2 * GROUP - 1) * H, H), :], sems.at[1]
    )

    @pl.when(flags[4] == 0)
    def _():
        hold[0] = above_ref[...].astype(F32)
        first.start()

    @pl.when(flags[5] == 0)
    def _():
        hold[1] = below_ref[...].astype(F32)
        last.start()

    @pl.when(flags[4] == 0)
    def _():
        first.wait()

    @pl.when(flags[5] == 0)
    def _():
        last.wait()


def settle(flags, main, above, below):
    return call(
        settle_body,
        flags,
        (above, below, main),
        [whole((H, N)), whole((H, N)), ANYWHERE],
        ANYWHERE,
        shape(GROUP * N, N, dtype=F32),
        (1,),
        scratch=[pltpu.VMEM((2, H, N), F32), pltpu.SemaphoreType.DMA((2,))],
        input_output_aliases={3: 0},
        name="settle",
    )


def exchange_columns(halves):
    return (*halves, move(halves[0], COL_RIGHT), move(halves[1], COL_LEFT))


def steps(factor):
    x = lax.axis_index("x")
    yl = lax.axis_index("yl")
    yh = lax.axis_index("yh")
    z = lax.axis_index("z")
    core = lax.axis_index("core")
    r = 2 * x + yl
    c = 16 * yh + 2 * z + core
    dx = (x - c // 8) & 3
    dy = yl ^ ((c // 4) & 1)
    dz = (z - 2 * (r & 3)) & 7
    dyh = yh ^ (r // 4)
    flags = lax.dynamic_index_in_dim(
        jnp.asarray(flag_table()), r * COLS + c, 0, keepdims=False
    )

    cross_out, cross_last = cross_block(flags, factor)
    cross = move(cross_out, CROSS)
    *rot_one, to_right, to_left = solve_one(flags, factor)
    from_left = move(to_right, NEXT_DIAG)
    from_right = move(to_left, PREV_DIAG)

    def out_of_source(rot):
        near, far, near_t, far_t = rot
        held = jnp.where(dz < 2, near_t, move(far_t, SPREAD_TWO))
        start = jnp.where(dy == 0, near, move(far, YL_FROM_SOURCE))
        return start, held

    sent_one = out_of_source(rot_one)
    rot_two = solve_two(flags, to_right, to_left, from_left, from_right, cross, cross_last)
    sent_two = out_of_source(rot_two)
    start = jnp.stack([sent_one[0], sent_two[0]], 1)
    held = jnp.stack([sent_one[1], sent_two[1]], 1)

    nearer = move(held[1], SPREAD_ONE)
    fore = move(start[0], x_pairs((0,), 1))
    back = move(start[1], x_pairs((0,), -1))
    fore_message = jnp.where(dx == 0, start[1], fore)
    back_message = jnp.where(dx == 0, start[0], back)
    take = (dz == 7) | (dz == 2) | (dz == 5) | (dz == 4)
    piece = jnp.where(take, nearer, held[0])

    copied = move(piece, YH_COPY)
    fore_next = move(fore_message, x_pairs((0, 1), 1))
    back_next = move(back_message, x_pairs((0, 3), -1))
    low = jnp.where(
        dx == 0, start[0], jnp.where(dx == 1, fore, jnp.where(dx == 2, fore_next, back_next))
    )
    high = jnp.where(
        dx == 0, start[1], jnp.where(dx == 1, fore_next, jnp.where(dx == 2, back_next, back))
    )
    mine = jnp.stack([low, high])
    piece = jnp.where(dyh == 0, piece, copied)

    other = move(mine, YL_SWAP)
    ahead = [piece]
    behind = [piece]

    def ring():
        ahead.append(move(ahead[-1], z_pairs(1)))
        behind.append(move(behind[-1], z_pairs(-1)))

    ring()
    ring()
    cols = jnp.concatenate(
        [jnp.where(dy == 0, mine, other), jnp.where(dy == 0, other, mine)], 0
    )
    edge = right(flags, (factor,), cols, 0, EDGE)
    edge = exchange_columns(edge)
    ring()
    inner = right(flags, (factor,), cols, 0, INNER)
    inner = exchange_columns(inner)
    last = (move(ahead[3][0], z_pairs(1)), move(behind[3][1], z_pairs(-1)))
    edge = right(flags, edge, cols, 1, EDGE)
    edge = exchange_columns(edge)
    inner = right(flags, inner, cols, 1, INNER)
    inner = exchange_columns(inner)
    line = jnp.stack(
        [piece, *behind[1:], jnp.stack(last), ahead[3], ahead[2], ahead[1]]
    )
    rows = line, move(line, CORE_SWAP)

    main, down, up = left(flags, rows, 0, EDGE, edge)
    above = move(down, ROW_DOWN)
    below = move(up, ROW_UP)
    (main,) = left(flags, rows, 0, INNER, inner, target=main)
    out, down, up = left(flags, rows, 1, EDGE, (main,), (above, below))
    last_above = move(down, ROW_DOWN)
    last_below = move(up, ROW_UP)
    (out,) = left(flags, rows, 1, INNER, (main,), target=out)
    return settle(flags, out, last_above, last_below)


def solution(mesh):
    split = Mesh(mesh.devices.reshape(4, 2, 2, 8, 2), ALL)
    placed = P(ROW, COL)
    return jax.shard_map(
        steps, mesh=split, in_specs=(placed,), out_specs=placed, check_vma=False
    )
```

```python
import math

import jax
import jax.numpy as jnp
import numpy as np
from jax import lax
from jax.experimental import pallas as pl
from jax.experimental.pallas import tpu as pltpu
from jax.sharding import Mesh
from jax.sharding import PartitionSpec as P

N = 512
H = 256
Q = 128
ROWS = 8
COLS = 32
GROUP = 4
ROW = ("x", "yl")
COL = ("yh", "z", "core")
ALL = ROW + COL
BF = jnp.bfloat16
F32 = jnp.float32


def dev(r, c):
    return r * COLS + c


def row_of(x, yl):
    return 2 * x + yl


def col_of(yh, z, core):
    return 16 * yh + 2 * z + core


def move(value, pairs):
    return lax.ppermute(value, ALL, pairs)


GRID = [(r, c) for r in range(ROWS) for c in range(COLS)]


def col_offset(r, c):
    return (r // 2 - c // 8) % 4, (r % 2) ^ ((c // 4) % 2)


def row_offset(r, c):
    return ((c // 2) % 8 - 2 * (r % 4)) % 8, (c // 16) ^ (r // 4)


def flag_table():
    table = np.zeros((ROWS * COLS, 16), np.int32)
    for r, c in GRID:
        local = c - GROUP * r
        dx, dy = col_offset(r, c)
        dz, dyh = row_offset(r, c)
        table[dev(r, c), :12] = [
            min(max(local, 0), GROUP - 1),
            int(0 <= local < GROUP),
            int(c == 0),
            int(c == COLS - 1),
            int(r == 0),
            int(r == ROWS - 1),
            max(c - 2, 0) % GROUP,
            dz,
            c % 2,
            dx,
            dy,
            dyh,
        ]
    return table


def x_pairs(starts, step):
    pairs = []
    for r, c in GRID:
        dx, _ = col_offset(r, c)
        if dx in starts:
            x = (r // 2 + step) % 4
            pairs.append((dev(r, c), dev(row_of(x, r % 2), c)))
    return pairs


YL_FROM_SOURCE = [(dev(k // 4, k), dev((k // 4) ^ 1, k)) for k in range(COLS)]
YL_SWAP = [(dev(r, c), dev(r ^ 1, c)) for r, c in GRID]
CORE_SWAP = [(dev(r, c), dev(r, c ^ 1)) for r, c in GRID]


def z_pairs(step, starts=None, planes=(0, 1)):
    pairs = []
    for r, c in GRID:
        dz, dyh = row_offset(r, c)
        if (starts is None or dz in starts) and dyh in planes:
            z = ((c // 2) % 8 + step) % 8
            pairs.append((dev(r, c), dev(r, col_of(c // 16, z, c % 2))))
    return pairs


SPREAD_TWO = z_pairs(-2, (0,), (0,)) + z_pairs(2, (1,), (0,))
SPREAD_ONE = z_pairs(-1, (0, 6), (0,)) + z_pairs(1, (1, 3), (0,))
YH_COPY = [(dev(r, c), dev(r, c ^ 16)) for r, c in GRID if row_offset(r, c)[1] == 0]
NEXT_DIAG = [(dev(k // 4, k), dev((k + 1) // 4, k + 1)) for k in range(COLS - 1)]
PREV_DIAG = [(dev(k // 4, k), dev((k - 1) // 4, k - 1)) for k in range(1, COLS)]
CROSS = [(dev(max(k - 1, 0) // 4, k + 1), dev(k // 4, k)) for k in range(COLS - 1)]
COL_NEAR = CORE_SWAP
COL_FAR = [
    (dev(r, c), dev(r, c + 2 * (c % 2) - 1)) for r, c in GRID if 0 < c < COLS - 1
]
ROW_DOWN = [(dev(r, c), dev(r + 1, c)) for r, c in GRID if r + 1 < ROWS]
ROW_UP = [(dev(r, c), dev(r - 1, c)) for r, c in GRID if r > 0]


def mm(a, b):
    return jnp.dot(a, b, preferred_element_type=F32)


def mm_t(a, b):
    return lax.dot_general(a, b, (((0,), (0,)), ((), ())), preferred_element_type=F32)


def pair_solve(block):
    size = block.shape[0]
    step_size = 0.5 / math.sqrt(size)
    col = lax.broadcasted_iota(jnp.int32, (size, size), 1)
    row = lax.broadcasted_iota(jnp.int32, (size, size), 0)
    scale = (col - row).astype(F32) * (step_size / size)

    def small_part(current):
        skew = current * scale
        narrow = skew.astype(BF)
        excess = skew + skew.T + mm_t(narrow, narrow)
        return skew - 0.5 * (excess + mm(narrow, excess.astype(BF)))

    first = small_part(block)
    first_b = first.astype(BF)
    half_way = block + mm(block.astype(BF), first_b)
    current = half_way + mm_t(first_b, half_way.astype(BF))
    second = small_part(current)
    both = first + second + mm(first_b, second.astype(BF))
    return (both + (col == row).astype(F32)).astype(BF)


def store_rotation(rot, near_ref, far_ref, near_t_ref, far_t_ref):
    turned = rot.T
    for p in range(2):
        near_ref[p] = rot[p * Q : (p + 1) * Q]
        far_ref[p] = rot[H + p * Q : H + (p + 1) * Q]
        near_t_ref[p] = turned[p * Q : (p + 1) * Q]
        far_t_ref[p] = turned[H + p * Q : H + (p + 1) * Q]


def solve_one_body(
    flags, matrix_ref, near, far, near_t, far_t, right_ref, left_ref, hold, sem
):
    @pl.when(flags[1] == 1)
    def _():
        fetched(matrix_ref, flags[0], hold, sem)
        block = hold[...]
        rot = pair_solve(block)
        store_rotation(rot, near, far, near_t, far_t)
        part = mm(block.astype(BF), rot).astype(BF)
        turned = mm_t(rot, part).astype(BF)
        first = flags[2] == 1
        up = jnp.concatenate([rot[:, :H], turned[:H, :H]], 0)
        low = jnp.concatenate([rot[:, H:], turned[H:, H:]], 0)
        right_ref[...] = jnp.where(first, low, up)
        left_ref[...] = jnp.where(first, up, low)


def solve_two_body(
    flags, own_right, own_left, came_right, came_left, cross_ref, last_ref, *outs
):
    @pl.when(flags[1] == 1)
    def _():
        last = flags[3] == 1
        up = jnp.where(flags[2] == 1, own_left[...], came_right[...])
        low = jnp.where(last, own_right[...], came_left[...])
        cross = jnp.where(last, last_ref[...], cross_ref[...])
        mixed = mm_t(up[:N], mm(cross, low[:N]).astype(BF))
        block = jnp.concatenate(
            [
                jnp.concatenate([up[N:].astype(F32), mixed], 1),
                jnp.concatenate([mixed.T, low[N:].astype(F32)], 1),
            ],
            0,
        )
        store_rotation(pair_solve(block), *outs)


def whole(shape):
    return pl.BlockSpec(shape, lambda i, f: (0,) * len(shape))


ANYWHERE = pl.BlockSpec(memory_space=pl.ANY)
IN_HBM = pl.BlockSpec(memory_space=pltpu.MemorySpace.HBM)
FETCH = [pltpu.VMEM((N, N), F32), pltpu.SemaphoreType.DMA]


def call(body, flags, args, in_specs, out_specs, out_shape, grid, scratch=(), **kw):
    return pl.pallas_call(
        body,
        grid_spec=pltpu.PrefetchScalarGridSpec(
            num_scalar_prefetch=1,
            grid=grid,
            in_specs=in_specs,
            out_specs=out_specs,
            scratch_shapes=scratch,
        ),
        out_shape=out_shape,
        compiler_params=pltpu.CompilerParams(dimension_semantics=("arbitrary",), vmem_limit_bytes=24 << 20
        ),
        **kw,
    )(flags, *args)


def shape(*dims, dtype=BF):
    return jax.ShapeDtypeStruct(dims, dtype)


def solve_one(flags, matrix):
    return call(
        solve_one_body,
        flags,
        (matrix,),
        [IN_HBM],
        [whole((2, Q, N))] * 4 + [whole((N + H, H))] * 2,
        [shape(2, Q, N)] * 4 + [shape(N + H, H)] * 2,
        (1,),
        scratch=FETCH,
        name="solve_one",
    )


def solve_two(flags, right, left, came_right, came_left, cross, last):
    message = whole((N + H, H))
    return call(
        solve_two_body,
        flags,
        (right, left, came_right, came_left, cross, last),
        [message] * 4 + [whole((N, N))] * 2,
        [whole((2, Q, N))] * 4,
        [shape(2, Q, N)] * 4,
        (1,),
        name="solve_two",
    )


def fetched(matrix_ref, slot, hold, sem):
    copy = pltpu.make_async_copy(matrix_ref.at[pl.ds(slot * N, N), :], hold, sem)
    copy.start()
    copy.wait()


def cast_body(flags, matrix_ref, out_ref, last_ref, hold, sem):
    fetched(matrix_ref, flags[6], hold, sem)
    out_ref[...] = hold[...].astype(BF)

    @pl.when(flags[3] == 1)
    def _():
        fetched(matrix_ref, GROUP - 2, hold, sem)
        last_ref[...] = hold[...].astype(BF)


def cross_block(flags, matrix):
    return call(
        cast_body,
        flags,
        (matrix,),
        [IN_HBM],
        [whole((N, N))] * 2,
        [shape(N, N)] * 2,
        (1,),
        scratch=FETCH,
        name="cross_block",
    )


EDGE = (0, 3)
INNER = (1, 1)


def store_halves(flags, product, near_ref, far_ref):
    up = product[:, :H]
    low = product[:, H:]
    low_first = jnp.logical_or(flags[2] == 1, flags[8] == 1)
    near_ref[...] = jnp.where(low_first, low, up)
    far_ref[...] = jnp.where(low_first, up, low)


def joined(flags, own_far, got_near, got_far):
    at_end = jnp.logical_or(flags[2] == 1, flags[3] == 1)
    far = jnp.where(at_end, own_far[...], got_far[...])
    near = got_near[...]
    odd = flags[8] == 1
    return jnp.concatenate([jnp.where(odd, near, far), jnp.where(odd, far, near)], 1)


def half_specs():
    return [
        pl.BlockSpec((N, H), lambda i, f: (i * (f[2] + f[3]), 0)),
        pl.BlockSpec((N, H), lambda i, f: (i, 0)),
        pl.BlockSpec((N, H), lambda i, f: (i, 0)),
    ]


def right_one_body(flags, block_ref, rot_ref, right_ref, left_ref):
    product = mm(block_ref[...].astype(BF), rot_ref[...].reshape(N, N)).astype(BF)
    store_halves(flags, product, right_ref, left_ref)


def right_two_body(flags, *refs):
    rot_ref, right_ref, left_ref = refs[3:]
    product = mm(joined(flags, *refs[:3]), rot_ref[...].reshape(N, N)).astype(BF)
    store_halves(flags, product, right_ref, left_ref)


def right(flags, sources, rot, slot, pairs):
    base, stride = pairs
    out = pl.BlockSpec((N, H), lambda i, f: (i, 0))
    first = slot == 0
    return call(
        right_one_body if first else right_two_body,
        flags,
        (*sources, rot),
        (
            [pl.BlockSpec((N, N), lambda i, f: (base + stride * i, 0))]
            if first
            else half_specs()
        )
        + [pl.BlockSpec((4, 1, Q, N), lambda i, f: (0, slot, 0, 0))],
        [out, out],
        [shape(2 * N, H)] * 2,
        (2,),
        name="right",
    )


def row_rotation(flags, i, mine, theirs):
    own_line = (i % 2) == flags[8]
    lower = i // 2
    parts = []
    for p in range(4):
        owner = jnp.where(lower == 1, 1 + p, (8 - p) % 8)
        spot = lax.rem(owner + 8 - flags[7], 8)
        parts.append(jnp.where(own_line, mine[spot, 0], theirs[spot, 0]))
    return jnp.concatenate(parts, 0)


def with_ends(flags, step, main_ref, above_ref, below_ref):
    block = main_ref[...]
    take_above = jnp.logical_and(step == 0, flags[4] == 0)
    take_below = jnp.logical_and(step == 1, flags[5] == 0)
    above = jnp.where(take_above, above_ref[...], block[:H])
    below = jnp.where(take_below, below_ref[...], block[H:])
    return jnp.concatenate([above, below], 0)


def left_body(pairs, slot, flags, *refs):
    base, stride = pairs
    step = pl.program_id(0)
    edge = pairs == EDGE
    mine, theirs = refs[:2]
    if slot == 0:
        block = joined(flags, *refs[2:5])
        rest = refs[5:]
    elif edge:
        block = with_ends(flags, step, *refs[2:5])
        rest = refs[5:]
    else:
        block = refs[2][...]
        rest = refs[3:]
    if edge:
        out_ref, down_ref, up_ref, hold, sems = rest
    else:
        out_ref, hold, sems = rest[1:]
    i = base + stride * step
    product = mm(row_rotation(flags, i, mine, theirs), block)
    up = product[:H].astype(hold.dtype)
    low = product[H:].astype(hold.dtype)
    hold[2 * step] = up
    hold[2 * step + 1] = low
    if edge:
        top = flags[4]
        up_spot = jnp.where(step == 0, 2 - 2 * top, 7)
        low_spot = jnp.where(step == 0, 2 * top, 5)

        @pl.when(step == 0)
        def _():
            up_ref[...] = low.astype(BF)

        @pl.when(step == 1)
        def _():
            down_ref[...] = up.astype(BF)
    else:
        up_spot = 2 * i + 2
        low_spot = 2 * i - 1

    def copies(s, up_at, low_at):
        return (
            pltpu.make_async_copy(
                hold.at[2 * s], out_ref.at[pl.ds(up_at * H, H), :], sems.at[2 * s]
            ),
            pltpu.make_async_copy(
                hold.at[2 * s + 1], out_ref.at[pl.ds(low_at * H, H), :], sems.at[2 * s + 1]
            ),
        )

    for copy in copies(step, up_spot, low_spot):
        copy.start()

    @pl.when(step == 1)
    def _():
        for s in range(2):
            for copy in copies(s, s, s):
                copy.wait()


def left(flags, rows, slot, pairs, sources, ends=(), target=None):
    base, stride = pairs
    edge = pairs == EDGE
    pieces = pl.BlockSpec((8, 1, Q, N), lambda i, f: (0, slot, 0, 0))
    if slot == 0:
        specs = half_specs()
    else:
        specs = [pl.BlockSpec((N, N), lambda i, f: (base + stride * i, 0))]
    specs = specs + [whole((H, N))] * len(ends)
    dtype = BF if slot == 0 else F32
    args = (*rows, *sources, *ends)
    return call(
        lambda *refs: left_body(pairs, slot, *refs),
        flags,
        args if edge else (*args, target),
        [pieces, pieces, *specs] + ([] if edge else [ANYWHERE]),
        [ANYWHERE] + ([whole((H, N))] * 2 if edge else []),
        [shape(GROUP * N, N, dtype=dtype)] + ([shape(H, N)] * 2 if edge else []),
        (2,),
        scratch=[pltpu.VMEM((4, H, N), dtype), pltpu.SemaphoreType.DMA((4,))],
        input_output_aliases={} if edge else {len(args) + 1: 0},
        name="left_edge" if edge else "left_inner",
    )


def settle_body(flags, above_ref, below_ref, main_ref, out_ref, hold, sems):
    first = pltpu.make_async_copy(hold.at[0], out_ref.at[pl.ds(0, H), :], sems.at[0])
    last = pltpu.make_async_copy(
        hold.at[1], out_ref.at[pl.ds((2 * GROUP - 1) * H, H), :], sems.at[1]
    )

    @pl.when(flags[4] == 0)
    def _():
        hold[0] = above_ref[...].astype(F32)
        first.start()

    @pl.when(flags[5] == 0)
    def _():
        hold[1] = below_ref[...].astype(F32)
        last.start()

    @pl.when(flags[4] == 0)
    def _():
        first.wait()

    @pl.when(flags[5] == 0)
    def _():
        last.wait()


def settle(flags, main, above, below):
    return call(
        settle_body,
        flags,
        (above, below, main),
        [whole((H, N)), whole((H, N)), ANYWHERE],
        ANYWHERE,
        shape(GROUP * N, N, dtype=F32),
        (1,),
        scratch=[pltpu.VMEM((2, H, N), F32), pltpu.SemaphoreType.DMA((2,))],
        input_output_aliases={3: 0},
        name="settle",
    )


def exchange_columns(halves):
    near, far = halves
    return far, move(near, COL_NEAR), move(far, COL_FAR)


def steps(factor):
    x = lax.axis_index("x")
    yl = lax.axis_index("yl")
    yh = lax.axis_index("yh")
    z = lax.axis_index("z")
    core = lax.axis_index("core")
    r = 2 * x + yl
    c = 16 * yh + 2 * z + core
    dx = (x - c // 8) & 3
    dy = yl ^ ((c // 4) & 1)
    dz = (z - 2 * (r & 3)) & 7
    dyh = yh ^ (r // 4)
    flags = lax.dynamic_index_in_dim(
        jnp.asarray(flag_table()), r * COLS + c, 0, keepdims=False
    )

    cross_out, cross_last = cross_block(flags, factor)
    cross = move(cross_out, CROSS)
    *rot_one, to_right, to_left = solve_one(flags, factor)
    from_left = move(to_right, NEXT_DIAG)
    from_right = move(to_left, PREV_DIAG)

    def out_of_source(rot):
        near, far, near_t, far_t = rot
        held = jnp.where(dz < 2, near_t, move(far_t, SPREAD_TWO))
        start = jnp.where(dy == 0, near, move(far, YL_FROM_SOURCE))
        return start, held

    sent_one = out_of_source(rot_one)
    rot_two = solve_two(flags, to_right, to_left, from_left, from_right, cross, cross_last)
    sent_two = out_of_source(rot_two)
    start = jnp.stack([sent_one[0], sent_two[0]], 1)
    held = jnp.stack([sent_one[1], sent_two[1]], 1)

    nearer = move(held[1], SPREAD_ONE)
    fore = move(start[0], x_pairs((0,), 1))
    back = move(start[1], x_pairs((0,), -1))
    fore_message = jnp.where(dx == 0, start[1], fore)
    back_message = jnp.where(dx == 0, start[0], back)
    take = (dz == 7) | (dz == 2) | (dz == 5) | (dz == 4)
    piece = jnp.where(take, nearer, held[0])

    copied = move(piece, YH_COPY)
    fore_next = move(fore_message, x_pairs((0, 1), 1))
    back_next = move(back_message, x_pairs((0, 3), -1))
    low = jnp.where(
        dx == 0, start[0], jnp.where(dx == 1, fore, jnp.where(dx == 2, fore_next, back_next))
    )
    high = jnp.where(
        dx == 0, start[1], jnp.where(dx == 1, fore_next, jnp.where(dx == 2, back_next, back))
    )
    mine = jnp.stack([low, high])
    piece = jnp.where(dyh == 0, piece, copied)

    other = move(mine, YL_SWAP)
    ahead = [piece]
    behind = [piece]

    def ring():
        ahead.append(move(ahead[-1], z_pairs(1)))
        behind.append(move(behind[-1], z_pairs(-1)))

    ring()
    ring()
    cols = jnp.concatenate(
        [jnp.where(dy == 0, mine, other), jnp.where(dy == 0, other, mine)], 0
    )
    edge = right(flags, (factor,), cols, 0, EDGE)
    edge = exchange_columns(edge)
    ring()
    inner = right(flags, (factor,), cols, 0, INNER)
    inner = exchange_columns(inner)
    last = (move(ahead[3][0], z_pairs(1)), move(behind[3][1], z_pairs(-1)))
    edge = right(flags, edge, cols, 1, EDGE)
    edge = exchange_columns(edge)
    inner = right(flags, inner, cols, 1, INNER)
    inner = exchange_columns(inner)
    line = jnp.stack(
        [piece, *behind[1:], jnp.stack(last), ahead[3], ahead[2], ahead[1]]
    )
    rows = line, move(line, CORE_SWAP)

    main, down, up = left(flags, rows, 0, EDGE, edge)
    above = move(down, ROW_DOWN)
    below = move(up, ROW_UP)
    (main,) = left(flags, rows, 0, INNER, inner, target=main)
    out, down, up = left(flags, rows, 1, EDGE, (main,), (above, below))
    last_above = move(down, ROW_DOWN)
    last_below = move(up, ROW_UP)
    (out,) = left(flags, rows, 1, INNER, (main,), target=out)
    return settle(flags, out, last_above, last_below)


def solution(mesh):
    split = Mesh(mesh.devices.reshape(4, 2, 2, 8, 2), ALL)
    placed = P(ROW, COL)
    return jax.shard_map(
        steps, mesh=split, in_specs=(placed,), out_specs=placed, check_vma=False
    )
```
